1024 devices in a mesh: circ: 64 (over x_lo, z, core), span: 16 (over x_hi, y).
Axes of the slice: x: 4 (x_hi: 2, x_lo: 2; x = x_hi * 2 + x_lo), y: 8, z: 16, core: 2. Of those that a mesh axis runs over, the one named last changes fastest.
Arguments:
- adjoint_rotor: float32 [6, 32, 4, 16384], P(None, 'span', None, 'circ'), may hold values from -6 to 6
- adjoint_stator: float32 [6, 32, 4, 16384], P(None, 'span', None, 'circ'), may hold values from -6 to 6
- jac_diag_rotor: float32 [6, 32, 4, 16384], P(None, 'span', None, 'circ'), may hold values from 2 to 4
- jac_diag_stator: float32 [6, 32, 4, 16384], P(None, 'span', None, 'circ'), may hold values from 2 to 4
- jac_off_rotor: bfloat16 [6, 6, 32, 4, 16384], P(None, None, 'span', None, 'circ'), may hold values from -1 to 1
- jac_off_stator: bfloat16 [6, 6, 32, 4, 16384], P(None, None, 'span', None, 'circ'), may hold values from -1 to 1
- source_rotor: float32 [6, 32, 4, 16384], P(None, 'span', None, 'circ'), may hold values from -6 to 6
- source_stator: float32 [6, 32, 4, 16384], P(None, 'span', None, 'circ'), may hold values from -6 to 6
- rotor_state: bfloat16 [6, 32, 16384], P(None, 'span', 'circ'), may hold values from -6 to 6
- margin_block: int32 [32, 128, 4], P('span'), may hold values from 0 to 127, as said below
- face_count: int32 [32, 128], P('span'), may hold values from 1 to 4
- margin_weight: float32 [32, 128, 4, 128], P('span'), may hold values from 0.2 to 1
Outputs:
- rotor_adjoint: float32 [6, 32, 4, 16384], P(None, 'span', None, 'circ')
- stator_adjoint: float32 [6, 32, 4, 16384], P(None, 'span', None, 'circ')
The draws below stay inside these ranges and needn't reach their ends.
Inputs may be any that keep to these rules, and one draw needn't show every extreme that they name: `margin_block`: entry k of the list of stator block b in spanwise row s is rotor block (b + o + 2 * 2 * s + 1 + j + k) mod 128, with one o for the whole array and j from 0 to 2 for each block of each row.
All inputs are finite; a program needn't handle non-finite values.
Results may differ from the reference program's by a relative error of at most 0.00055.
Values may be sent and summed in bfloat16 or wider, within the bound.
A program may use at most 32 MiB of HBM per device.

```python
import jax
import jax.numpy as jnp
from jax import lax

VARS = 6
LAYERS = 4
BLOCKS_DEV = 2
BLOCK = 128
MARGINS = 4
STEPS = 2
SPANS = 32
BLOCKS = 128
CELLS = 16384


def draw_margin_block(key, part):
    rotation = jax.random.randint(jax.random.fold_in(key, 11), (), 0, BLOCKS, dtype=jnp.int32)
    jitter = jax.random.randint(jax.random.fold_in(key, 12), (SPANS, BLOCKS, 1), 0, 3, dtype=jnp.int32)
    lean = (2 * BLOCKS_DEV * jnp.arange(SPANS, dtype=jnp.int32) + BLOCKS_DEV - 1)[:, None, None]
    stator_blocks = jnp.arange(BLOCKS, dtype=jnp.int32)[None, :, None]
    entries = jnp.arange(MARGINS, dtype=jnp.int32)[None, None, :]
    return ((stator_blocks + rotation + lean + jitter + entries) % BLOCKS).astype(jnp.int32)


def with_ends(values, stream_key, low, top_value):
    longest = values.shape.index(max(values.shape))
    spots = []
    for shift in (0, 1):
        where = [jax.random.randint(jax.random.fold_in(stream_key, axis), (), 0, length) for axis, length in enumerate(values.shape)]
        where[longest] = (where[longest] + shift) % values.shape[longest]
        spots.append(tuple(where))
    return values.at[spots[0]].set(low).at[spots[1]].set(top_value)


def block_scale(own_key, dims, shards, smallest, largest):
    def one(dim, blocks):
        heights = jax.random.uniform(jax.random.fold_in(jax.random.fold_in(own_key, 6), dim), (blocks,), jnp.float32, smallest / len(shards), largest / len(shards))
        return jnp.repeat(jnp.exp(heights), dims[dim] // blocks).reshape((-1,) + (1,) * (len(dims) - dim - 1))

    factor_of = one(*shards[0])
    for cut in shards[1:]:
        factor_of = factor_of * one(*cut)
    return factor_of


def gaussian(stream_key, dims, scale, limit, cuts=(), kind=jnp.bfloat16):
    result = scale * jax.random.normal(stream_key, dims, jnp.float32)
    if cuts:
        result = result * block_scale(stream_key, dims, cuts, -0.22, 0.18)
    return jnp.clip(result, -limit, limit).astype(kind)


def setup_inputs(seed: int = 0) -> dict:
    key_list = jax.random.split(jax.random.key(seed), 13)
    adjoint_rotor = gaussian(key_list[0], (VARS, SPANS, LAYERS, CELLS), 1.0, 6.0, ((1, 16), (3, 64)), jnp.float32)
    adjoint_stator = gaussian(key_list[1], (VARS, SPANS, LAYERS, CELLS), 1.0, 6.0, ((1, 16), (3, 64)), jnp.float32)
    jac_diag_rotor = jnp.clip(2.0 + 2.0 * jax.random.uniform(key_list[2], (VARS, SPANS, LAYERS, CELLS), jnp.float32) ** block_scale(key_list[2], (VARS, SPANS, LAYERS, CELLS), ((1, 16), (3, 64)), -0.2, 0.2), 2.0, 4.0)
    jac_diag_stator = jnp.clip(2.0 + 2.0 * jax.random.uniform(key_list[3], (VARS, SPANS, LAYERS, CELLS), jnp.float32) ** block_scale(key_list[3], (VARS, SPANS, LAYERS, CELLS), ((1, 16), (3, 64)), -0.2, 0.2), 2.0, 4.0)
    jac_off_rotor = gaussian(key_list[4], (VARS, VARS, SPANS, LAYERS, CELLS), 0.3, 1.0, ((2, 16), (4, 64)))
    jac_off_stator = gaussian(key_list[5], (VARS, VARS, SPANS, LAYERS, CELLS), 0.3, 1.0, ((2, 16), (4, 64)))
    source_rotor = gaussian(key_list[6], (VARS, SPANS, LAYERS, CELLS), 1.0, 6.0, ((1, 16), (3, 64)), jnp.float32)
    source_stator = gaussian(key_list[7], (VARS, SPANS, LAYERS, CELLS), 1.0, 6.0, ((1, 16), (3, 64)), jnp.float32)
    rotor_state = gaussian(key_list[8], (VARS, SPANS, CELLS), 1.0, 6.0, ((1, 16), (2, 64)))
    margin_block = draw_margin_block(jax.random.fold_in(key_list[12], 71), 0)
    face_count = with_ends(jax.random.randint(key_list[10], (SPANS, BLOCKS), 1, MARGINS + 1), jax.random.fold_in(key_list[10], 1), 1, MARGINS).astype(jnp.int32)
    margin_weight = jnp.clip(0.2 + 0.8 * jax.random.uniform(key_list[11], (SPANS, BLOCKS, MARGINS, BLOCK), jnp.float32) ** block_scale(key_list[11], (SPANS, BLOCKS, MARGINS, BLOCK), ((0, 16),), -0.2, 0.2), 0.2, 1.0)
    return dict(adjoint_rotor=adjoint_rotor, adjoint_stator=adjoint_stator, jac_diag_rotor=jac_diag_rotor, jac_diag_stator=jac_diag_stator, jac_off_rotor=jac_off_rotor, jac_off_stator=jac_off_stator, source_rotor=source_rotor, source_stator=source_stator, rotor_state=rotor_state, margin_block=margin_block, face_count=face_count, margin_weight=margin_weight)


step_size = 0.1
coupling = 0.2

def interface_flux(primal, adjoint):
    speeds = jnp.sqrt(1.0 + primal * primal)
    projection = lax.optimization_barrier(jnp.sum(primal * adjoint, axis=0)) / (6.0 + lax.optimization_barrier(jnp.sum(primal * primal, axis=0)))
    return speeds * adjoint + 0.5 * primal * projection[None]

def jacobian_apply(jac_diag, jac_off, adjoint):
    applied = jac_diag * adjoint
    for source_var in range(adjoint.shape[0]):
        applied = applied + jac_off[source_var].astype(jnp.float32) * adjoint[source_var][None]
    return applied

def neighbours(adjoint):
    beside_all = jnp.roll(adjoint, 1, axis=3) + jnp.roll(adjoint, -1, axis=3)
    layer_pad = jnp.pad(adjoint, ((0, 0), (0, 0), (1, 1), (0, 0)))
    beside_all = beside_all + layer_pad[:, :, 2:] + layer_pad[:, :, :-2]
    span_pad = jnp.pad(adjoint, ((0, 0), (1, 1), (0, 0), (0, 0)))
    return beside_all + span_pad[:, 2:] + span_pad[:, :-2]

def reference(adjoint_rotor, adjoint_stator, jac_diag_rotor, jac_diag_stator, jac_off_rotor, jac_off_stator, source_rotor, source_stator, rotor_state, margin_block, face_count, margin_weight):
    live_mask = (jnp.arange(MARGINS, dtype=jnp.int32)[None, None, :] < face_count[:, :, None]).astype(jnp.float32)
    weights_live = margin_weight * live_mask[:, :, :, None]
    rotor_blocks = rotor_state.astype(jnp.float32).reshape(VARS, SPANS, BLOCKS, BLOCK)
    span_index = jnp.arange(SPANS, dtype=jnp.int32)[:, None]
    stator_primal = jnp.zeros((VARS, SPANS, BLOCKS, BLOCK), jnp.float32)
    for column in range(MARGINS):
        picked = rotor_blocks[:, span_index, margin_block[:, :, column], :]
        stator_primal = stator_primal + weights_live[None, :, :, column, :] * picked
    stator_primal = stator_primal.reshape(VARS, SPANS, CELLS)
    rotor_adj, stator_adj = (adjoint_rotor, adjoint_stator)
    for sweep in range(STEPS):
        face_flux = interface_flux(stator_primal, stator_adj[:, :, 0, :])
        flux_wire = lax.optimization_barrier(face_flux.astype(jnp.bfloat16)).astype(jnp.float32)
        flux_blocks = flux_wire.reshape(VARS, SPANS, BLOCKS, BLOCK)
        pulled = jnp.zeros((VARS, SPANS, BLOCKS, BLOCK), jnp.float32)
        for column in range(MARGINS):
            pulled = pulled.at[:, span_index, margin_block[:, :, column], :].add(weights_live[None, :, :, column, :] * flux_blocks)
        pulled = pulled.reshape(VARS, SPANS, CELLS)
        rotor_res = jacobian_apply(jac_diag_rotor, jac_off_rotor, rotor_adj) - coupling * neighbours(rotor_adj) - source_rotor
        rotor_res = rotor_res.at[:, :, LAYERS - 1, :].add(-pulled)
        stator_res = jacobian_apply(jac_diag_stator, jac_off_stator, stator_adj) - coupling * neighbours(stator_adj) - source_stator
        stator_res = stator_res.at[:, :, 0, :].add(face_flux)
        rotor_adj = rotor_adj - step_size * rotor_res
        stator_adj = stator_adj - step_size * stator_res
    return (rotor_adj, stator_adj)
```

```python
import functools

import jax
import jax.numpy as jnp
from jax import lax
from jax.experimental import pallas as pl
from jax.experimental.pallas import tpu as pltpu
from jax.sharding import PartitionSpec as P

STEPS = 2
STEP_SIZE = 0.1
COUPLING = 0.2
COARSE = 8
REACH = 3
LOW = COARSE // 2 + REACH
SLOTS = COARSE + 2 * REACH
HIGH = SLOTS - 1 - LOW


def kernel(
    ring,
    band,
    adj_r,
    adj_s,
    diag_r,
    diag_s,
    off_r,
    off_s,
    src_r,
    src_s,
    rstate,
    margin,
    count,
    weight,
    out_r,
    out_s,
    adj,
    diag,
    off,
    src,
    wts,
    lists,
    live,
    pick,
    pad,
    part,
    adj1,
    edge,
    rows,
    near_a,
    near_b,
    near_f,
    sent_f,
    prim,
    face,
    flux,
    far_a0,
    far_a1,
    far_b,
    far_f,
    sent_b,
    pull,
    in_sem,
    out_sem,
    edge_sem,
    near_sem,
    far_sem,
    send_sem,
):
    far_a = (far_a0, far_a1)
    c = lax.axis_index("circ")
    s = lax.axis_index("span")

    def circ(shift):
        return {"circ": lax.rem(c + (shift + ring), ring)}

    def span(shift):
        return {"span": lax.rem(s + (shift + band), band)}

    def remote(source, target, sent, landed, where):
        return pltpu.make_async_remote_copy(
            src_ref=source,
            dst_ref=target,
            send_sem=sent,
            recv_sem=landed,
            device_id=where,
            device_id_type=pl.DeviceIdType.MESH,
        )

    loads = [
        (margin, lists),
        (count, live),
        (adj_r, adj.at[0]),
        (adj_s, adj.at[1]),
        (rstate, pick),
        (off_r, off.at[0]),
        (off_s, off.at[1]),
        (diag_r, diag.at[0]),
        (diag_s, diag.at[1]),
        (src_r, src.at[0]),
        (src_s, src.at[1]),
        (weight, wts),
    ]
    copies = [pltpu.make_async_copy(a, b, in_sem.at[i]) for i, (a, b) in enumerate(loads)]
    for one in copies:
        one.start()

    barrier = pltpu.get_barrier_semaphore()

    def greet(where):
        pl.semaphore_signal(
            barrier, inc=1, device_id=where, device_id_type=pl.DeviceIdType.MESH
        )

    for shift in range(1, COARSE):
        greet(circ(shift))
        greet(circ(-shift))
    for shift in range(COARSE, ring, COARSE):
        greet(circ(shift))
    greet(span(1))
    greet(span(-1))

    def coarse(piece, landing, sign, landed, sent):
        @pl.loop(1, COARSE)
        def _(a):
            remote(piece, landing.at[a], sent, landed, circ(sign * COARSE * a)).start()

    def fine(piece, landing, sign, landed, sent):
        @pl.loop(1, HIGH + 1)
        def _(t):
            remote(piece, landing.at[t], sent, landed, circ(sign * t)).start()

        @pl.loop(1, LOW + 1)
        def _(t):
            remote(piece, landing.at[SLOTS - t], sent, landed, circ(-sign * t)).start()

    def drain(view, sem):
        pltpu.make_async_copy(view, view, sem).wait()

    def edges(source, step, first, last):
        lower = source.at[first:last, :, :, :, pl.ds(0, 128)]
        upper = source.at[first:last, :, :, :, pl.ds(128, 128)]
        sems = edge_sem.at[step, first]
        return [
            remote(upper, edge.at[step, 0, first:last], sems.at[4], sems.at[0], circ(1)),
            remote(lower, edge.at[step, 1, first:last], sems.at[5], sems.at[1], circ(-1)),
            remote(
                source.at[first:last, :, 1],
                rows.at[step, 0, first:last],
                sems.at[6],
                sems.at[2],
                span(1),
            ),
            remote(
                source.at[first:last, :, 0],
                rows.at[step, 1, first:last],
                sems.at[7],
                sems.at[3],
                span(-1),
            ),
        ]

    pad[...] = jnp.zeros_like(pad)
    copies[2].wait()
    copies[3].wait()
    pl.semaphore_wait(barrier, 2 * (COARSE - 1) + ring // COARSE - 1 + 2)

    coarse(rstate, near_a, -1, near_sem.at[0], send_sem.at[0])
    first_edges = edges(adj, 0, 0, 2)
    for one in first_edges:
        one.start()

    copies[0].wait()
    copies[1].wait()
    base = lists[0, 0, 0]
    shift = lax.shift_right_logical(base, 1) + 2
    fine_at = ((shift + COARSE // 2) & (COARSE - 1)) - COARSE // 2
    coarse_at = lax.shift_right_logical(shift - fine_at + ring, 3) & (COARSE - 1)

    copies[4].wait()
    near_a[0] = pick[...]
    drain(near_a.at[pl.ds(1, COARSE - 1)], near_sem.at[0])
    chosen = near_a[coarse_at]
    sent_f[...] = chosen
    near_b[0] = chosen
    fine(sent_f, near_b, -1, near_sem.at[1], send_sem.at[1])

    def local_part(x, field):
        pad[field, :, :, 1:5, :] = x[...]
        value = diag[field] * x[...] - src[field]
        value = value - COUPLING * (pad[field, :, :, 0:4, :] + pad[field, :, :, 2:6, :])

        def add(w, total):
            return total + off[field, w].astype(jnp.float32) * x[w][None]

        part[field] = lax.fori_loop(0, off.shape[1], add, value)

    lane = lax.broadcasted_iota(jnp.int32, (1, 1, 1, 128), 3)
    below = jnp.where(s == 0, 0.0, 1.0).astype(jnp.float32)
    above = jnp.where(s == band - 1, 0.0, 1.0).astype(jnp.float32)

    def advance(x, result, field, step):
        for half in range(2):
            here = pl.ds(half * 128, 128)
            other = pl.ds(128 - half * 128, 128)
            mine = x[:, :, :, here]
            before = edge[step, 0, field] if half == 0 else x[:, :, :, other]
            after = x[:, :, :, other] if half == 0 else edge[step, 1, field]
            left = pltpu.roll(jnp.where(lane == 127, before, mine), 1, axis=3)
            right = pltpu.roll(jnp.where(lane == 0, after, mine), 127, axis=3)
            beside = left + right
            spanwise0 = rows[step, 0, field, :, :, here] * below + x[:, 1, :, here]
            spanwise1 = rows[step, 1, field, :, :, here] * above + x[:, 0, :, here]
            whole = part[field, :, :, :, here] - COUPLING * beside
            result[:, 0, :, here] = mine[:, 0] - STEP_SIZE * (whole[:, 0] - COUPLING * spanwise0)
            result[:, 1, :, here] = mine[:, 1] - STEP_SIZE * (whole[:, 1] - COUPLING * spanwise1)

    for one in copies[5:]:
        one.wait()
    for field in (1, 0):
        local_part(adj.at[field], field)
    for one in first_edges:
        one.wait()
    for field in (1, 0):
        advance(adj.at[field], adj1.at[field], field, 0)

    drain(near_b.at[pl.ds(1, SLOTS - 1)], near_sem.at[1])
    for half in range(2):
        near_f[:, half] = near_b[:, :, :, pl.ds(half * 128, 128)].astype(jnp.float32)

    def spot(delta, sign):
        delta = (delta + 2 * REACH) & (2 * ring - 1)
        w = lax.shift_right_logical(delta, 1) - REACH
        t = fine_at + sign * w
        t = t + (SLOTS & lax.shift_right_arithmetic(t, 31))
        return jnp.minimum(t, SLOTS - 1), delta & 1

    def masked(factor, k, alive):
        shape = factor.shape
        return jnp.where(jnp.full(shape, k) < jnp.full(shape, alive), factor, 0.0)

    for row in range(2):
        for block in range(2):
            b = 2 * c + block
            head = lists[row, 0, b]
            alive = live[row, b]
            total = jnp.zeros((6, 1, 128), jnp.float32)
            for k in range(4):
                slot, half = spot(head + k - 2 * c - 2 * shift, 1)
                got = near_f[slot, half, :, row : row + 1, :]
                total = total + masked(wts[row, b, k : k + 1, :], k, alive)[None] * got
            prim[:, row : row + 1, pl.ds(block * 128, 128)] = total

    for row in range(2):
        face[:, row : row + 1, :] = adj[1, :, row, 0:1, :]
    q = prim[...]
    speeds = jnp.sqrt(1.0 + q * q)
    norm = 6.0 + jnp.sum(q * q, axis=0)

    def interface_flux(p):
        projection = jnp.sum(q * p, axis=0) / norm
        return speeds * p + 0.5 * q * projection[None]

    for step in range(STEPS):
        value = interface_flux(face[...])
        flux[...] = value
        wire = value.astype(jnp.bfloat16)
        sent_b[step, 0] = wire
        far_a[step][0] = wire
        coarse(sent_b.at[step, 0], far_a[step], 1, far_sem.at[step, 0], send_sem.at[2 + 2 * step])
        if step == 0:
            for row in range(2):
                first = adj1[1, :, row, 0:1, :] - STEP_SIZE * flux[:, row : row + 1, :]
                adj1[1, :, row, 0:1, :] = first
                face[:, row : row + 1, :] = first

    stator_edges = edges(adj1, 1, 1, 2)
    for one in stator_edges:
        one.start()

    for step in range(STEPS):
        drain(far_a[step].at[pl.ds(1, COARSE - 1)], far_sem.at[step, 0])
        chosen = far_a[step][coarse_at]
        sent_b[step, 1] = chosen
        far_b[step, 0] = chosen
        fine(sent_b.at[step, 1], far_b.at[step], 1, far_sem.at[step, 1], send_sem.at[3 + 2 * step])

    local_part(adj1.at[1], 1)
    for one in stator_edges:
        one.wait()
    advance(adj1.at[1], adj.at[1], 1, 1)
    for row in range(2):
        adj[1, :, row, 0:1, :] = adj[1, :, row, 0:1, :] - STEP_SIZE * flux[:, row : row + 1, :]
    store_s = pltpu.make_async_copy(adj.at[1], out_s, out_sem.at[0])
    store_s.start()

    def pulled(step):
        drain(far_b.at[step, pl.ds(1, SLOTS - 1)], far_sem.at[step, 1])
        for half in range(2):
            far_f[:, half] = far_b[step, :, :, :, pl.ds(half * 128, 128)].astype(jnp.float32)
        for row in range(2):
            for block in range(2):
                r = 2 * c + block
                total = jnp.zeros((6, 1, 128), jnp.float32)
                for m in range(-2, 6):
                    b = (r - base - 4 * row - m + 4 * ring) & (2 * ring - 1)
                    k = (r - lists[row, 0, b] + 2 * ring) & (2 * ring - 1)
                    slot, half = spot(b - 2 * c + 2 * shift, -1)
                    got = far_f[slot, half, :, row : row + 1, :]
                    factor = wts[row, b, pl.ds(jnp.minimum(k, 3), 1), :]
                    total = total + masked(factor, k, live[row, b])[None] * got
                pull[:, row : row + 1, pl.ds(block * 128, 128)] = total

    pulled(0)
    for row in range(2):
        adj1[0, :, row, 3:4, :] = adj1[0, :, row, 3:4, :] + STEP_SIZE * pull[:, row : row + 1, :]
    rotor_edges = edges(adj1, 1, 0, 1)
    for one in rotor_edges:
        one.start()
    local_part(adj1.at[0], 0)
    pulled(1)
    for one in rotor_edges:
        one.wait()
    advance(adj1.at[0], adj.at[0], 0, 1)
    for row in range(2):
        adj[0, :, row, 3:4, :] = adj[0, :, row, 3:4, :] + STEP_SIZE * pull[:, row : row + 1, :]
    store_r = pltpu.make_async_copy(adj.at[0], out_r, out_sem.at[1])
    store_r.start()

    drain(near_a.at[pl.ds(1, COARSE - 1)], send_sem.at[0])
    drain(near_b.at[pl.ds(1, SLOTS - 1)], send_sem.at[1])
    for step in range(STEPS):
        drain(far_a[step].at[pl.ds(1, COARSE - 1)], send_sem.at[2 + 2 * step])
        drain(far_b.at[step, pl.ds(1, SLOTS - 1)], send_sem.at[3 + 2 * step])
    store_s.wait()
    store_r.wait()


def solution(mesh):
    ring, band = mesh.shape["circ"], mesh.shape["span"]

    def per_device(
        adjoint_rotor,
        adjoint_stator,
        jac_diag_rotor,
        jac_diag_stator,
        jac_off_rotor,
        jac_off_stator,
        source_rotor,
        source_stator,
        rotor_state,
        margin_block,
        face_count,
        margin_weight,
    ):
        f32, bf16 = jnp.float32, jnp.bfloat16
        shape = adjoint_rotor.shape
        piece = rotor_state.shape
        lists = jnp.transpose(margin_block, (0, 2, 1))
        out = jax.ShapeDtypeStruct(shape, f32)
        hbm = pl.BlockSpec(memory_space=pltpu.HBM)
        return pl.pallas_call(
            functools.partial(kernel, ring, band),
            out_shape=(out, out),
            in_specs=[hbm] * 12,
            out_specs=(hbm, hbm),
            scratch_shapes=[
                pltpu.VMEM((2,) + shape, f32),
                pltpu.VMEM((2,) + shape, f32),
                pltpu.VMEM((2,) + jac_off_rotor.shape, bf16),
                pltpu.VMEM((2,) + shape, f32),
                pltpu.VMEM(margin_weight.shape, f32),
                pltpu.SMEM(lists.shape, jnp.int32),
                pltpu.SMEM(face_count.shape, jnp.int32),
                pltpu.VMEM(piece, bf16),
                pltpu.VMEM((2, 6, 2, 8, 256), f32),
                pltpu.VMEM((2,) + shape, f32),
                pltpu.VMEM((2,) + shape, f32),
                pltpu.VMEM((STEPS, 2, 2, 6, 2, 4, 128), f32),
                pltpu.VMEM((STEPS, 2, 2, 6, 4, 256), f32),
                pltpu.VMEM((COARSE,) + piece, bf16),
                pltpu.VMEM((SLOTS,) + piece, bf16),
                pltpu.VMEM((SLOTS, 2, 6, 2, 128), f32),
                pltpu.VMEM(piece, bf16),
                pltpu.VMEM(piece, f32),
                pltpu.VMEM(piece, f32),
                pltpu.VMEM(piece, f32),
                pltpu.VMEM((COARSE,) + piece, bf16),
                pltpu.VMEM((COARSE,) + piece, bf16),
                pltpu.VMEM((STEPS, SLOTS) + piece, bf16),
                pltpu.VMEM((SLOTS, 2, 6, 2, 128), f32),
                pltpu.VMEM((STEPS, 2) + piece, bf16),
                pltpu.VMEM(piece, f32),
                pltpu.SemaphoreType.DMA((12,)),
                pltpu.SemaphoreType.DMA((2,)),
                pltpu.SemaphoreType.DMA((STEPS, 2, 8)),
                pltpu.SemaphoreType.DMA((2,)),
                pltpu.SemaphoreType.DMA((STEPS, 2)),
                pltpu.SemaphoreType.DMA((6,)),
            ],
            compiler_params=pltpu.CompilerParams(
                collective_id=0, has_side_effects=True, vmem_limit_bytes=60 * 1024 * 1024
            ),
            name="sweep",
        )(
            adjoint_rotor,
            adjoint_stator,
            jac_diag_rotor,
            jac_diag_stator,
            jac_off_rotor,
            jac_off_stator,
            source_rotor,
            source_stator,
            rotor_state,
            lists,
            face_count,
            margin_weight,
        )

    field = P(None, "span", None, "circ")
    matrix = P(None, None, "span", None, "circ")
    placed = (field,) * 4 + (matrix,) * 2 + (field,) * 2
    placed = placed + (
        P(None, "span", "circ"),
        P("span", None, None),
        P("span", None),
        P("span", None, None, None),
    )
    return jax.shard_map(
        per_device, mesh=mesh, in_specs=placed, out_specs=(field, field), check_vma=False
    )
```

```python
import functools

import jax
import jax.numpy as jnp
from jax import lax
from jax.experimental import pallas as pl
from jax.experimental.pallas import tpu as pltpu
from jax.sharding import PartitionSpec as P

STEPS = 2
STEP_SIZE = 0.1
COUPLING = 0.2
COARSE = 8
STRIDE = 8
OFFSET = 4
REACH = 6
SLOTS = 2 * REACH + 1
BESIDE = 3
HOMES = 2 * BESIDE + 1
SEEN = 7


def kernel(
    ring,
    band,
    adj_r,
    adj_s,
    diag_r,
    diag_s,
    off_r,
    off_s,
    src_r,
    src_s,
    rstate,
    margin,
    count,
    weight,
    out_r,
    out_s,
    adj,
    diag,
    off,
    src,
    wts,
    lists,
    live,
    pick,
    pad,
    part,
    adj1,
    edge,
    rows,
    home,
    home_f,
    near_a,
    near_b,
    near_f,
    sent_n,
    prim,
    face,
    flux,
    far_a0,
    far_a1,
    far_b0,
    far_b1,
    sent_f,
    qtab,
    ptab,
    wtab,
    pull,
    in_sem,
    out_sem,
    edge_sem,
    land_sem,
    send_sem,
):
    c = lax.axis_index("circ")
    s = lax.axis_index("span")
    blocks = 2 * ring

    def circ(shift):
        return {"circ": lax.rem(c + (shift + ring), ring)}

    def span(shift):
        return {"span": lax.rem(s + (shift + band), band)}

    def remote(source, target, sent, landed, where):
        return pltpu.make_async_remote_copy(
            src_ref=source,
            dst_ref=target,
            send_sem=sent,
            recv_sem=landed,
            device_id=where,
            device_id_type=pl.DeviceIdType.MESH,
        )

    loads = [
        (adj_s, adj.at[1]),
        (adj_r, adj.at[0]),
        (margin, lists),
        (count, live),
        (off_s, off.at[1]),
        (diag_s, diag.at[1]),
        (src_s, src.at[1]),
        (off_r, off.at[0]),
        (diag_r, diag.at[0]),
        (src_r, src.at[0]),
        (rstate, pick),
        (weight, wts),
    ]
    copies = [pltpu.make_async_copy(a, b, in_sem.at[i]) for i, (a, b) in enumerate(loads)]
    for one in copies:
        one.start()

    barrier = pltpu.get_barrier_semaphore()

    def greet(where):
        pl.semaphore_signal(
            barrier, inc=1, device_id=where, device_id_type=pl.DeviceIdType.MESH
        )

    far = [x for x in range(OFFSET, ring, STRIDE) if REACH < x < ring - REACH]
    for shift in far + list(range(1, REACH + 1)) + list(range(-REACH, 0)):
        greet(circ(shift))
    greet(span(1))
    greet(span(-1))

    def coarse(piece, landing, sign, n):
        @pl.loop(0, COARSE)
        def _(a):
            away = sign * (STRIDE * a + OFFSET)
            remote(piece, landing.at[a], send_sem.at[n], land_sem.at[n], circ(away)).start()

    def fine(piece, landing, sign, n):
        @pl.loop(1, REACH + 1)
        def _(t):
            remote(piece, landing.at[t], send_sem.at[n], land_sem.at[n], circ(sign * t)).start()
            low = landing.at[SLOTS - t]
            remote(piece, low, send_sem.at[n], land_sem.at[n], circ(-sign * t)).start()

    def drain(view, sem):
        pltpu.make_async_copy(view, view, sem).wait()

    def edges(source, step, field):
        lower = source.at[field, :, :, :, pl.ds(0, 128)]
        upper = source.at[field, :, :, :, pl.ds(128, 128)]
        sems = edge_sem.at[step, field]
        return [
            remote(upper, edge.at[step, 0, field], sems.at[4], sems.at[0], circ(1)),
            remote(lower, edge.at[step, 1, field], sems.at[5], sems.at[1], circ(-1)),
            remote(
                source.at[field, :, 1], rows.at[step, 0, field], sems.at[6], sems.at[2], span(1)
            ),
            remote(
                source.at[field, :, 0], rows.at[step, 1, field], sems.at[7], sems.at[3], span(-1)
            ),
        ]

    def begin(copies):
        for one in copies:
            one.start()
        return copies

    def finish(copies):
        for one in copies:
            one.wait()

    def front(target, source, row, half):
        target[half, :, row : row + 1, :] = source[1, :, row, 0:1, pl.ds(half * 128, 128)]

    pieces = [(row, half) for row in range(2) for half in range(2)]
    pad[...] = jnp.zeros_like(pad)
    qtab[...] = jnp.zeros_like(qtab)
    ptab[...] = jnp.zeros_like(ptab)
    wtab[...] = jnp.zeros_like(wtab)
    copies[0].wait()
    for row, half in pieces:
        front(sent_f.at[0], adj, row, half)
    copies[1].wait()
    pl.semaphore_wait(barrier, len(far) + 2 * REACH + 2)

    coarse(rstate, near_a, -1, 0)
    coarse(sent_f.at[0], far_a0, 1, 1)
    edges0_s = begin(edges(adj, 0, 1))

    @pl.loop(1, BESIDE + 1)
    def _(u):
        remote(rstate, home.at[u], send_sem.at[6], land_sem.at[6], circ(-u)).start()
        remote(rstate, home.at[HOMES - u], send_sem.at[6], land_sem.at[6], circ(u)).start()

    edges0_r = begin(edges(adj, 0, 0))

    def local_part(x, field):
        pad[field, :, :, 1:5, :] = x[...]
        value = diag[field] * x[...] - src[field]
        value = value - COUPLING * (pad[field, :, :, 0:4, :] + pad[field, :, :, 2:6, :])

        def add(w, total):
            return total + off[field, w].astype(jnp.float32) * x[w][None]

        part[field] = lax.fori_loop(0, off.shape[1], add, value)

    lane = lax.broadcasted_iota(jnp.int32, (1, 1, 1, 128), 3)
    below = jnp.where(s == 0, 0.0, 1.0).astype(jnp.float32)
    above = jnp.where(s == band - 1, 0.0, 1.0).astype(jnp.float32)

    def advance(x, result, field, step):
        for half in range(2):
            here = pl.ds(half * 128, 128)
            other = pl.ds(128 - half * 128, 128)
            mine = x[:, :, :, here]
            before = edge[step, 0, field] if half == 0 else x[:, :, :, other]
            after = x[:, :, :, other] if half == 0 else edge[step, 1, field]
            left = pltpu.roll(jnp.where(lane == 127, before, mine), 1, axis=3)
            right = pltpu.roll(jnp.where(lane == 0, after, mine), 127, axis=3)
            beside = left + right
            spanwise0 = rows[step, 0, field, :, :, here] * below + x[:, 1, :, here]
            spanwise1 = rows[step, 1, field, :, :, here] * above + x[:, 0, :, here]
            whole = part[field, :, :, :, here] - COUPLING * beside
            result[:, 0, :, here] = mine[:, 0] - STEP_SIZE * (whole[:, 0] - COUPLING * spanwise0)
            result[:, 1, :, here] = mine[:, 1] - STEP_SIZE * (whole[:, 1] - COUPLING * spanwise1)

    for one in copies[4:7]:
        one.wait()
    local_part(adj.at[1], 1)
    finish(edges0_s)
    advance(adj.at[1], adj1.at[1], 1, 0)
    for row, half in pieces:
        front(sent_f.at[1], adj1, row, half)
    coarse(sent_f.at[1], far_a1, 1, 2)

    copies[2].wait()
    copies[3].wait()
    start = lists[0, 0, 0]

    def lowest(b, least):
        for row in range(2):
            e = ((lists[row, 0, b] - b - 4 * row - start + 2 + blocks) & (blocks - 1)) - 2
            least = jnp.minimum(least, e)
        return least

    base = (start + lax.fori_loop(0, blocks, lowest, jnp.int32(0)) + blocks) & (blocks - 1)
    shift = lax.shift_right_logical(base, 1) + 3
    fine_at = ((shift - 1) & 7) - 3
    coarse_at = lax.shift_right_logical(shift - fine_at - OFFSET, 3) & 7

    drain(near_a, land_sem.at[0])
    chosen = near_a[coarse_at]
    sent_n[...] = chosen
    near_b[0] = chosen
    fine(sent_n, near_b, -1, 3)
    drain(far_a0, land_sem.at[1])
    chosen = far_a0[coarse_at]
    sent_f[2] = chosen
    far_b0[0] = chosen
    fine(sent_f.at[2], far_b0, 1, 4)

    for one in copies[7:]:
        one.wait()
    local_part(adj.at[0], 0)
    finish(edges0_r)
    advance(adj.at[0], adj1.at[0], 0, 0)

    def wrap(t, size):
        t = t + (size & lax.shift_right_arithmetic(t, 31))
        return jnp.minimum(t, size - 1)

    def masked(factor, k, alive):
        shape = factor.shape
        return jnp.where(jnp.full(shape, k) < jnp.full(shape, alive), factor, 0.0)

    home[0] = pick[...]
    drain(home.at[pl.ds(1, HOMES - 1)], land_sem.at[6])
    for half in range(2):
        home_f[:, half] = home[:, :, :, pl.ds(half * 128, 128)].astype(jnp.float32)

    places = [(row, i) for row in range(2) for i in range(SEEN)]
    owners = []
    for row, i in places:
        b = (2 * c + 1 - base - 4 * row - i + 2 * blocks) & (blocks - 1)
        owners.append(b)
        first = lists[row, 0, b]
        alive = live[row, b]
        total = jnp.zeros((6, 1, 128), jnp.float32)
        for k in range(4):
            near = (first + k - 2 * c + 2 * BESIDE + blocks) & (blocks - 1)
            u = wrap(lax.shift_right_logical(near, 1) - BESIDE, HOMES)
            got = home_f[u, near & 1, :, row : row + 1, :]
            total = total + masked(wts[row, b, k : k + 1, :], k, alive)[None] * got
        qtab[row, :, i : i + 1, :] = total
        for block in range(2):
            if not 0 <= i - 1 + block < SEEN - 1:
                continue
            k = (2 * c + block - first + blocks) & (blocks - 1)
            factor = wts[row, b, pl.ds(jnp.minimum(k, 3), 1), :]
            wtab[row, block, i : i + 1, :] = masked(factor, k, alive)

    drain(far_a1, land_sem.at[2])
    chosen = far_a1[coarse_at]
    sent_f[3] = chosen
    far_b1[0] = chosen
    fine(sent_f.at[3], far_b1, 1, 5)

    def gather(landing):
        for (row, i), b in zip(places, owners):
            delta = (b - 2 * c + 2 * shift + 4 + blocks) & (blocks - 1)
            slot = wrap(fine_at - lax.shift_right_logical(delta, 1) + 2, SLOTS)
            ptab[row, :, i : i + 1, :] = landing[slot, delta & 1, :, row : row + 1, :]

    def speeds_of(q):
        return jnp.sqrt(1.0 + q * q)

    def interface_flux(q, p, axis):
        projection = jnp.sum(q * p, axis=axis, keepdims=True)
        projection = projection / (6.0 + jnp.sum(q * q, axis=axis, keepdims=True))
        return speeds_of(q) * p + 0.5 * q * projection

    def pulled(value):
        wire = value.astype(jnp.bfloat16).astype(jnp.float32)
        for row in range(2):
            for block in range(2):
                total = jnp.sum(wtab[row, block][None] * wire[row], axis=1, keepdims=True)
                pull[:, row : row + 1, pl.ds(block * 128, 128)] = total

    drain(far_b0.at[pl.ds(1, SLOTS - 1)], land_sem.at[4])
    gather(far_b0)
    first_flux = interface_flux(qtab[...], ptab[...], 1)
    pulled(first_flux)
    for row in range(2):
        adj1[0, :, row, 3:4, :] = adj1[0, :, row, 3:4, :] + STEP_SIZE * pull[:, row : row + 1, :]
    edges1_r = begin(edges(adj1, 1, 0))
    ptab[...] = STEP_SIZE * first_flux
    qtab1 = qtab

    drain(near_b.at[pl.ds(1, SLOTS - 1)], land_sem.at[3])
    for half in range(2):
        near_f[:, half] = near_b[:, :, :, pl.ds(half * 128, 128)].astype(jnp.float32)
    for row in range(2):
        for block in range(2):
            b = 2 * c + block
            first = lists[row, 0, b]
            alive = live[row, b]
            total = jnp.zeros((6, 1, 128), jnp.float32)
            for k in range(4):
                delta = (first + k - 2 * c - 2 * shift + 6 + 2 * blocks) & (blocks - 1)
                slot = wrap(fine_at + lax.shift_right_logical(delta, 1) - 3, SLOTS)
                got = near_f[slot, delta & 1, :, row : row + 1, :]
                total = total + masked(wts[row, b, k : k + 1, :], k, alive)[None] * got
            prim[:, row : row + 1, pl.ds(block * 128, 128)] = total
    for row in range(2):
        face[:, row : row + 1, :] = adj[1, :, row, 0:1, :]
    value = STEP_SIZE * interface_flux(prim[...], face[...], 0)
    flux[...] = value
    for row in range(2):
        moved = adj1[1, :, row, 0:1, :] - flux[:, row : row + 1, :]
        adj1[1, :, row, 0:1, :] = moved
        face[:, row : row + 1, :] = moved
    edges1_s = begin(edges(adj1, 1, 1))
    flux[...] = STEP_SIZE * interface_flux(prim[...], face[...], 0)

    local_part(adj1.at[0], 0)
    local_part(adj1.at[1], 1)

    finish(edges1_s)
    advance(adj1.at[1], adj.at[1], 1, 1)
    for row in range(2):
        adj[1, :, row, 0:1, :] = adj[1, :, row, 0:1, :] - flux[:, row : row + 1, :]
    store_s = pltpu.make_async_copy(adj.at[1], out_s, out_sem.at[0])
    store_s.start()

    finish(edges1_r)
    advance(adj1.at[0], adj.at[0], 0, 1)
    scaled = ptab[...]
    drain(far_b1.at[pl.ds(1, SLOTS - 1)], land_sem.at[5])
    gather(far_b1)
    pulled(interface_flux(qtab1[...], ptab[...] - scaled, 1))
    for row in range(2):
        adj[0, :, row, 3:4, :] = adj[0, :, row, 3:4, :] + STEP_SIZE * pull[:, row : row + 1, :]
    store_r = pltpu.make_async_copy(adj.at[0], out_r, out_sem.at[1])
    store_r.start()

    drain(near_a, send_sem.at[0])
    drain(far_a0, send_sem.at[1])
    drain(far_a1, send_sem.at[2])
    drain(near_b.at[pl.ds(1, SLOTS - 1)], send_sem.at[3])
    drain(far_b0.at[pl.ds(1, SLOTS - 1)], send_sem.at[4])
    drain(far_b1.at[pl.ds(1, SLOTS - 1)], send_sem.at[5])
    drain(home.at[pl.ds(1, HOMES - 1)], send_sem.at[6])
    store_s.wait()
    store_r.wait()


def solution(mesh):
    ring, band = mesh.shape["circ"], mesh.shape["span"]

    def per_device(
        adjoint_rotor,
        adjoint_stator,
        jac_diag_rotor,
        jac_diag_stator,
        jac_off_rotor,
        jac_off_stator,
        source_rotor,
        source_stator,
        rotor_state,
        margin_block,
        face_count,
        margin_weight,
    ):
        f32, bf16 = jnp.float32, jnp.bfloat16
        shape = adjoint_rotor.shape
        piece = rotor_state.shape
        split = (2, 6, 2, 128)
        lists = jnp.transpose(margin_block, (0, 2, 1))
        out = jax.ShapeDtypeStruct(shape, f32)
        hbm = pl.BlockSpec(memory_space=pltpu.HBM)
        return pl.pallas_call(
            functools.partial(kernel, ring, band),
            out_shape=(out, out),
            in_specs=[hbm] * 12,
            out_specs=(hbm, hbm),
            scratch_shapes=[
                pltpu.VMEM((2,) + shape, f32),
                pltpu.VMEM((2,) + shape, f32),
                pltpu.VMEM((2,) + jac_off_rotor.shape, bf16),
                pltpu.VMEM((2,) + shape, f32),
                pltpu.VMEM(margin_weight.shape, f32),
                pltpu.SMEM(lists.shape, jnp.int32),
                pltpu.SMEM(face_count.shape, jnp.int32),
                pltpu.VMEM(piece, bf16),
                pltpu.VMEM((2, 6, 2, 8, 256), f32),
                pltpu.VMEM((2,) + shape, f32),
                pltpu.VMEM((2,) + shape, f32),
                pltpu.VMEM((STEPS, 2, 2, 6, 2, 4, 128), f32),
                pltpu.VMEM((STEPS, 2, 2, 6, 4, 256), f32),
                pltpu.VMEM((HOMES,) + piece, bf16),
                pltpu.VMEM((HOMES,) + split, f32),
                pltpu.VMEM((COARSE,) + piece, bf16),
                pltpu.VMEM((SLOTS,) + piece, bf16),
                pltpu.VMEM((SLOTS,) + split, f32),
                pltpu.VMEM(piece, bf16),
                pltpu.VMEM(piece, f32),
                pltpu.VMEM(piece, f32),
                pltpu.VMEM(piece, f32),
                pltpu.VMEM((COARSE,) + split, f32),
                pltpu.VMEM((COARSE,) + split, f32),
                pltpu.VMEM((SLOTS,) + split, f32),
                pltpu.VMEM((SLOTS,) + split, f32),
                pltpu.VMEM((4,) + split, f32),
                pltpu.VMEM((2, 6, 8, 128), f32),
                pltpu.VMEM((2, 6, 8, 128), f32),
                pltpu.VMEM((2, 2, 8, 128), f32),
                pltpu.VMEM(piece, f32),
                pltpu.SemaphoreType.DMA((12,)),
                pltpu.SemaphoreType.DMA((2,)),
                pltpu.SemaphoreType.DMA((STEPS, 2, 8)),
                pltpu.SemaphoreType.DMA((7,)),
                pltpu.SemaphoreType.DMA((7,)),
            ],
            compiler_params=pltpu.CompilerParams(
                collective_id=0, has_side_effects=True, vmem_limit_bytes=60 * 1024 * 1024
            ),
            name="sweep",
        )(
            adjoint_rotor,
            adjoint_stator,
            jac_diag_rotor,
            jac_diag_stator,
            jac_off_rotor,
            jac_off_stator,
            source_rotor,
            source_stator,
            rotor_state,
            lists,
            face_count,
            margin_weight,
        )

    field = P(None, "span", None, "circ")
    matrix = P(None, None, "span", None, "circ")
    placed = (field,) * 4 + (matrix,) * 2 + (field,) * 2
    placed = placed + (
        P(None, "span", "circ"),
        P("span", None, None),
        P("span", None),
        P("span", None, None, None),
    )
    return jax.shard_map(
        per_device, mesh=mesh, in_specs=placed, out_specs=(field, field), check_vma=False
    )
```

```python
import functools

import jax
import jax.numpy as jnp
from jax import lax
from jax.experimental import pallas as pl
from jax.experimental.pallas import tpu as pltpu
from jax.sharding import PartitionSpec as P

STEPS = 2
STEP_SIZE = 0.1
COUPLING = 0.2
COARSE = 8
STRIDE = 8
OFFSET = 4
REACH = 6
SLOTS = 2 * REACH + 1
COMMON = 4
FILLED = REACH + COMMON
BESIDE = 3
HOMES = 2 * BESIDE + 1
SEEN = 7


def kernel(
    ring,
    band,
    adj_r,
    adj_s,
    diag_r,
    diag_s,
    off_r,
    off_s,
    src_r,
    src_s,
    rstate,
    margin,
    count,
    weight,
    out_r,
    out_s,
    adj,
    diag,
    off,
    src,
    wts,
    lists,
    live,
    pick,
    pad,
    part,
    adj1,
    edge,
    rows,
    home,
    home_f,
    near_a,
    near_b,
    near_f,
    sent_n,
    prim,
    face,
    flux,
    far_a0,
    far_a1,
    far_b0,
    far_b1,
    sent_f,
    sent_d,
    delta,
    far_f,
    side,
    brow,
    qtab,
    ptab,
    dtab,
    wtab,
    pull,
    in_sem,
    out_sem,
    edge_sem,
    land_sem,
    send_sem,
    tip_sem,
):
    c = lax.axis_index("circ")
    s = lax.axis_index("span")
    blocks = 2 * ring

    def circ(shift):
        return {"circ": lax.rem(c + (shift + ring), ring)}

    def span(shift):
        return {"span": lax.rem(s + (shift + band), band)}

    def remote(source, target, sent, landed, where):
        return pltpu.make_async_remote_copy(
            src_ref=source,
            dst_ref=target,
            send_sem=sent,
            recv_sem=landed,
            device_id=where,
            device_id_type=pl.DeviceIdType.MESH,
        )

    barrier = pltpu.get_barrier_semaphore()

    def greet(where):
        pl.semaphore_signal(
            barrier, inc=1, device_id=where, device_id_type=pl.DeviceIdType.MESH
        )

    far = [x for x in range(OFFSET, ring, STRIDE) if REACH < x < ring - REACH]
    for shift in far + list(range(1, REACH + 1)) + list(range(-REACH, 0)):
        greet(circ(shift))
    greet(span(1))
    greet(span(-1))

    loads = [
        (adj_s, adj.at[1]),
        (adj_r, adj.at[0]),
        (margin, lists),
        (count, live),
        (off_s, off.at[1]),
        (diag_s, diag.at[1]),
        (src_s, src.at[1]),
        (off_r, off.at[0]),
        (diag_r, diag.at[0]),
        (src_r, src.at[0]),
        (rstate, pick),
        (weight, wts),
    ]
    copies = [pltpu.make_async_copy(a, b, in_sem.at[i]) for i, (a, b) in enumerate(loads)]
    for one in copies:
        one.start()

    def coarse(piece, landing, sign, n):
        @pl.loop(0, COARSE)
        def _(a):
            away = sign * (STRIDE * a + OFFSET)
            remote(piece, landing.at[a], send_sem.at[n], land_sem.at[n], circ(away)).start()

    def fine(piece, landing, sign, n):
        @pl.loop(1, REACH + 1)
        def _(t):
            remote(piece, landing.at[t], send_sem.at[n], land_sem.at[n], circ(sign * t)).start()
            low = landing.at[SLOTS - t]
            remote(piece, low, send_sem.at[n], land_sem.at[n], circ(-sign * t)).start()

    def fine_rows(piece, landing, n):
        def go(row, slot, away):
            source = piece if row is None else piece.at[row]
            target = landing.at[slot] if row is None else landing.at[slot, row]
            remote(source, target, send_sem.at[n], land_sem.at[n], circ(away)).start()

        @pl.loop(1, COMMON + 1)
        def _(t):
            go(None, t, t)
            go(None, SLOTS - t, -t)

        @pl.loop(COMMON + 1, REACH + 1)
        def _(t):
            go(1, t, t)
            go(0, SLOTS - t, -t)

    def drain(view, sem):
        pltpu.make_async_copy(view, view, sem).wait()

    def edges(source, step, field):
        lower = source.at[field, :, :, :, pl.ds(0, 128)]
        upper = source.at[field, :, :, :, pl.ds(128, 128)]
        sems = edge_sem.at[step, field]
        return [
            remote(upper, edge.at[step, 0, field], sems.at[4], sems.at[0], circ(1)),
            remote(lower, edge.at[step, 1, field], sems.at[5], sems.at[1], circ(-1)),
            remote(
                source.at[field, :, 1], rows.at[step, 0, field], sems.at[6], sems.at[2], span(1)
            ),
            remote(
                source.at[field, :, 0], rows.at[step, 1, field], sems.at[7], sems.at[3], span(-1)
            ),
        ]

    def begin(copies):
        for one in copies:
            one.start()
        return copies

    def finish(copies):
        for one in copies:
            one.wait()

    def front(target, source, row, half):
        target[row, :, half : half + 1, :] = source[1, :, row, 0:1, pl.ds(half * 128, 128)]

    pieces = [(row, half) for row in range(2) for half in range(2)]
    pad[...] = jnp.zeros_like(pad)
    qtab[...] = jnp.zeros_like(qtab)
    ptab[...] = jnp.zeros_like(ptab)
    dtab[...] = jnp.zeros_like(dtab)
    for landing in (far_b0, far_b1):
        for t in range(COMMON + 1, REACH + 1):
            landing[t, 0] = jnp.zeros_like(landing[t, 0])
            landing[SLOTS - t, 1] = jnp.zeros_like(landing[t, 0])
    wtab[...] = jnp.zeros_like(wtab)
    copies[0].wait()
    for row, half in pieces:
        front(sent_f.at[0], adj, row, half)
    copies[1].wait()
    pl.semaphore_wait(barrier, len(far) + 2 * REACH + 2)

    first = sent_f.at[0]
    tips = begin(
        [
            remote(first, side.at[0], tip_sem.at[4], tip_sem.at[0], circ(1)),
            remote(first, side.at[1], tip_sem.at[5], tip_sem.at[1], circ(-1)),
            remote(first.at[1], brow.at[0], tip_sem.at[6], tip_sem.at[2], span(1)),
            remote(first.at[0], brow.at[1], tip_sem.at[7], tip_sem.at[3], span(-1)),
        ]
    )
    coarse(first, far_a0, 1, 1)
    coarse(rstate, near_a, -1, 0)

    @pl.loop(1, BESIDE + 1)
    def _(u):
        remote(rstate, home.at[u], send_sem.at[6], land_sem.at[6], circ(-u)).start()
        remote(rstate, home.at[HOMES - u], send_sem.at[6], land_sem.at[6], circ(u)).start()

    edges0_s = begin(edges(adj, 0, 1))
    edges0_r = begin(edges(adj, 0, 0))

    def local_part(x, field):
        pad[field, :, :, 1:5, :] = x[...]
        value = diag[field] * x[...] - src[field]
        value = value - COUPLING * (pad[field, :, :, 0:4, :] + pad[field, :, :, 2:6, :])

        def add(w, total):
            return total + off[field, w].astype(jnp.float32) * x[w][None]

        part[field] = lax.fori_loop(0, off.shape[1], add, value)

    lane = lax.broadcasted_iota(jnp.int32, (1, 1, 1, 128), 3)
    below = jnp.where(s == 0, 0.0, 1.0).astype(jnp.float32)
    above = jnp.where(s == band - 1, 0.0, 1.0).astype(jnp.float32)

    def advance(x, result, field, step):
        for half in range(2):
            here = pl.ds(half * 128, 128)
            other = pl.ds(128 - half * 128, 128)
            mine = x[:, :, :, here]
            before = edge[step, 0, field] if half == 0 else x[:, :, :, other]
            after = x[:, :, :, other] if half == 0 else edge[step, 1, field]
            left = pltpu.roll(jnp.where(lane == 127, before, mine), 1, axis=3)
            right = pltpu.roll(jnp.where(lane == 0, after, mine), 127, axis=3)
            beside = left + right
            spanwise0 = rows[step, 0, field, :, :, here] * below + x[:, 1, :, here]
            spanwise1 = rows[step, 1, field, :, :, here] * above + x[:, 0, :, here]
            whole = part[field, :, :, :, here] - COUPLING * beside
            result[:, 0, :, here] = mine[:, 0] - STEP_SIZE * (whole[:, 0] - COUPLING * spanwise0)
            result[:, 1, :, here] = mine[:, 1] - STEP_SIZE * (whole[:, 1] - COUPLING * spanwise1)

    for one in copies[4:7]:
        one.wait()
    local_part(adj.at[1], 1)
    finish(tips)
    line = lax.broadcasted_iota(jnp.int32, (1, 1, 128), 2)
    for row, half in pieces:

        def mine(row, half):
            return sent_f[0, row, :, half : half + 1, :]

        x = mine(row, half)
        before = side[0, row, :, 1:2, :] if half == 0 else mine(row, 0)
        after = mine(row, 1) if half == 0 else side[1, row, :, 0:1, :]
        around = pltpu.roll(jnp.where(line == 127, before, x), 1, axis=2)
        around = around + pltpu.roll(jnp.where(line == 0, after, x), 127, axis=2)
        outer = brow[row, :, half : half + 1, :] * (below if row == 0 else above)
        around = around + outer + mine(1 - row, half)
        value = part[1, :, row, 0:1, pl.ds(half * 128, 128)] - COUPLING * around
        delta[row, :, half : half + 1, :] = -STEP_SIZE * value
    sent_d[0] = delta[...].astype(jnp.bfloat16)
    coarse(sent_d.at[0], far_a1, 1, 2)

    copies[2].wait()
    copies[3].wait()
    start = lists[0, 0, 0]

    def lowest(b, least):
        for row in range(2):
            e = ((lists[row, 0, b] - b - 4 * row - start + 2 + blocks) & (blocks - 1)) - 2
            least = jnp.minimum(least, e)
        return least

    base = (start + lax.fori_loop(0, blocks, lowest, jnp.int32(0), unroll=8) + blocks) & (blocks - 1)
    shift = lax.shift_right_logical(base, 1) + 3
    fine_at = ((shift - 1) & 7) - 3
    coarse_at = lax.shift_right_logical(shift - fine_at - OFFSET, 3) & 7

    drain(far_a0, land_sem.at[1])
    chosen = far_a0[coarse_at]
    sent_f[1] = chosen
    far_b0[0] = chosen
    fine_rows(sent_f.at[1], far_b0, 4)
    drain(near_a, land_sem.at[0])
    chosen = near_a[coarse_at]
    sent_n[...] = chosen
    near_b[0] = chosen
    fine(sent_n, near_b, -1, 3)

    finish(edges0_s)
    advance(adj.at[1], adj1.at[1], 1, 0)

    for one in copies[7:]:
        one.wait()
    local_part(adj.at[0], 0)
    finish(edges0_r)
    advance(adj.at[0], adj1.at[0], 0, 0)

    def wrap(t, size):
        t = t + (size & lax.shift_right_arithmetic(t, 31))
        return jnp.minimum(t, size - 1)

    def masked(factor, k, alive):
        shape = factor.shape
        return jnp.where(jnp.full(shape, k) < jnp.full(shape, alive), factor, 0.0)

    home[0] = pick[...]
    drain(home.at[pl.ds(1, HOMES - 1)], land_sem.at[6])
    for half in range(2):
        home_f[:, half] = home[:, :, :, pl.ds(half * 128, 128)].astype(jnp.float32)

    places = [(row, i) for row in range(2) for i in range(SEEN)]
    owners = []
    for row, i in places:
        b = (2 * c + 1 - base - 4 * row - i + 2 * blocks) & (blocks - 1)
        owners.append(b)
        first = lists[row, 0, b]
        alive = live[row, b]
        total = jnp.zeros((6, 1, 128), jnp.float32)
        for k in range(4):
            near = (first + k - 2 * c + 2 * BESIDE + blocks) & (blocks - 1)
            u = wrap(lax.shift_right_logical(near, 1) - BESIDE, HOMES)
            got = home_f[u, near & 1, :, row : row + 1, :]
            total = total + masked(wts[row, b, k : k + 1, :], k, alive)[None] * got
        qtab[row, :, i : i + 1, :] = total
        for block in range(2):
            if not 0 <= i - 1 + block < SEEN - 1:
                continue
            k = (2 * c + block - first + blocks) & (blocks - 1)
            factor = wts[row, b, pl.ds(jnp.minimum(k, 3), 1), :]
            wtab[row, block, i : i + 1, :] = masked(factor, k, alive)

    drain(far_a1, land_sem.at[2])
    chosen = far_a1[coarse_at]
    sent_d[1] = chosen
    far_b1[0] = chosen
    fine_rows(sent_d.at[1], far_b1, 5)

    def gather(landing, table):
        for (row, i), b in zip(places, owners):
            delta = (b - 2 * c + 2 * shift + 4 + blocks) & (blocks - 1)
            slot = wrap(fine_at - lax.shift_right_logical(delta, 1) + 2, SLOTS)
            table[row, :, i : i + 1, :] = landing[slot, row, :, pl.ds(delta & 1, 1), :]

    def speeds_of(q):
        return jnp.sqrt(1.0 + q * q)

    def interface_flux(q, p, axis):
        projection = jnp.sum(q * p, axis=axis, keepdims=True)
        projection = projection / (6.0 + jnp.sum(q * q, axis=axis, keepdims=True))
        return speeds_of(q) * p + 0.5 * q * projection

    def pulled(value):
        wire = value.astype(jnp.bfloat16).astype(jnp.float32)
        for row in range(2):
            for block in range(2):
                total = jnp.sum(wtab[row, block][None] * wire[row], axis=1, keepdims=True)
                pull[:, row : row + 1, pl.ds(block * 128, 128)] = total

    drain(far_b0.at[pl.ds(1, FILLED)], land_sem.at[4])
    gather(far_b0, ptab)
    first_flux = interface_flux(qtab[...], ptab[...], 1)
    pulled(first_flux)
    for row in range(2):
        adj1[0, :, row, 3:4, :] = adj1[0, :, row, 3:4, :] + STEP_SIZE * pull[:, row : row + 1, :]
    edges1_r = begin(edges(adj1, 1, 0))
    ptab[...] = ptab[...] - STEP_SIZE * first_flux

    drain(near_b.at[pl.ds(1, SLOTS - 1)], land_sem.at[3])
    for half in range(2):
        near_f[:, half] = near_b[:, :, :, pl.ds(half * 128, 128)].astype(jnp.float32)
    for row in range(2):
        for block in range(2):
            b = 2 * c + block
            first = lists[row, 0, b]
            alive = live[row, b]
            total = jnp.zeros((6, 1, 128), jnp.float32)
            for k in range(4):
                delta = (first + k - 2 * c - 2 * shift + 6 + 2 * blocks) & (blocks - 1)
                slot = wrap(fine_at + lax.shift_right_logical(delta, 1) - 3, SLOTS)
                got = near_f[slot, delta & 1, :, row : row + 1, :]
                total = total + masked(wts[row, b, k : k + 1, :], k, alive)[None] * got
            prim[:, row : row + 1, pl.ds(block * 128, 128)] = total
    for row in range(2):
        face[:, row : row + 1, :] = adj[1, :, row, 0:1, :]
    value = STEP_SIZE * interface_flux(prim[...], face[...], 0)
    flux[...] = value
    for row in range(2):
        moved = adj1[1, :, row, 0:1, :] - flux[:, row : row + 1, :]
        adj1[1, :, row, 0:1, :] = moved
        face[:, row : row + 1, :] = moved
    edges1_s = begin(edges(adj1, 1, 1))
    flux[...] = STEP_SIZE * interface_flux(prim[...], face[...], 0)

    local_part(adj1.at[0], 0)
    local_part(adj1.at[1], 1)

    finish(edges1_s)
    advance(adj1.at[1], adj.at[1], 1, 1)
    for row in range(2):
        adj[1, :, row, 0:1, :] = adj[1, :, row, 0:1, :] - flux[:, row : row + 1, :]
    store_s = pltpu.make_async_copy(adj.at[1], out_s, out_sem.at[0])
    store_s.start()

    finish(edges1_r)
    advance(adj1.at[0], adj.at[0], 0, 1)
    drain(far_b1.at[pl.ds(1, FILLED)], land_sem.at[5])
    far_f[...] = far_b1[...].astype(jnp.float32)
    gather(far_f, dtab)
    pulled(interface_flux(qtab[...], ptab[...] + dtab[...], 1))
    for row in range(2):
        adj[0, :, row, 3:4, :] = adj[0, :, row, 3:4, :] + STEP_SIZE * pull[:, row : row + 1, :]
    store_r = pltpu.make_async_copy(adj.at[0], out_r, out_sem.at[1])
    store_r.start()

    drain(near_a, send_sem.at[0])
    drain(far_a0, send_sem.at[1])
    drain(far_a1, send_sem.at[2])
    drain(near_b.at[pl.ds(1, SLOTS - 1)], send_sem.at[3])
    drain(far_b0.at[pl.ds(1, FILLED)], send_sem.at[4])
    drain(far_b1.at[pl.ds(1, FILLED)], send_sem.at[5])
    drain(home.at[pl.ds(1, HOMES - 1)], send_sem.at[6])
    store_s.wait()
    store_r.wait()


def solution(mesh):
    ring, band = mesh.shape["circ"], mesh.shape["span"]

    def per_device(
        adjoint_rotor,
        adjoint_stator,
        jac_diag_rotor,
        jac_diag_stator,
        jac_off_rotor,
        jac_off_stator,
        source_rotor,
        source_stator,
        rotor_state,
        margin_block,
        face_count,
        margin_weight,
    ):
        f32, bf16 = jnp.float32, jnp.bfloat16
        shape = adjoint_rotor.shape
        piece = rotor_state.shape
        split = (2, 6, 2, 128)
        lists = jnp.transpose(margin_block, (0, 2, 1))
        out = jax.ShapeDtypeStruct(shape, f32)
        hbm = pl.BlockSpec(memory_space=pltpu.HBM)
        return pl.pallas_call(
            functools.partial(kernel, ring, band),
            out_shape=(out, out),
            in_specs=[hbm] * 12,
            out_specs=(hbm, hbm),
            scratch_shapes=[
                pltpu.VMEM((2,) + shape, f32),
                pltpu.VMEM((2,) + shape, f32),
                pltpu.VMEM((2,) + jac_off_rotor.shape, bf16),
                pltpu.VMEM((2,) + shape, f32),
                pltpu.VMEM(margin_weight.shape, f32),
                pltpu.SMEM(lists.shape, jnp.int32),
                pltpu.SMEM(face_count.shape, jnp.int32),
                pltpu.VMEM(piece, bf16),
                pltpu.VMEM((2, 6, 2, 8, 256), f32),
                pltpu.VMEM((2,) + shape, f32),
                pltpu.VMEM((2,) + shape, f32),
                pltpu.VMEM((STEPS, 2, 2, 6, 2, 4, 128), f32),
                pltpu.VMEM((STEPS, 2, 2, 6, 4, 256), f32),
                pltpu.VMEM((HOMES,) + piece, bf16),
                pltpu.VMEM((HOMES,) + split, f32),
                pltpu.VMEM((COARSE,) + piece, bf16),
                pltpu.VMEM((SLOTS,) + piece, bf16),
                pltpu.VMEM((SLOTS,) + split, f32),
                pltpu.VMEM(piece, bf16),
                pltpu.VMEM(piece, f32),
                pltpu.VMEM(piece, f32),
                pltpu.VMEM(piece, f32),
                pltpu.VMEM((COARSE,) + split, f32),
                pltpu.VMEM((COARSE,) + split, bf16),
                pltpu.VMEM((SLOTS,) + split, f32),
                pltpu.VMEM((SLOTS,) + split, bf16),
                pltpu.VMEM((2,) + split, f32),
                pltpu.VMEM((2,) + split, bf16),
                pltpu.VMEM(split, f32),
                pltpu.VMEM((SLOTS,) + split, f32),
                pltpu.VMEM((2,) + split, f32),
                pltpu.VMEM((2,) + split[1:], f32),
                pltpu.VMEM((2, 6, 8, 128), f32),
                pltpu.VMEM((2, 6, 8, 128), f32),
                pltpu.VMEM((2, 6, 8, 128), f32),
                pltpu.VMEM((2, 2, 8, 128), f32),
                pltpu.VMEM(piece, f32),
                pltpu.SemaphoreType.DMA((12,)),
                pltpu.SemaphoreType.DMA((2,)),
                pltpu.SemaphoreType.DMA((STEPS, 2, 8)),
                pltpu.SemaphoreType.DMA((7,)),
                pltpu.SemaphoreType.DMA((7,)),
                pltpu.SemaphoreType.DMA((8,)),
            ],
            compiler_params=pltpu.CompilerParams(
                collective_id=0, has_side_effects=True, vmem_limit_bytes=60 * 1024 * 1024
            ),
            name="sweep",
        )(
            adjoint_rotor,
            adjoint_stator,
            jac_diag_rotor,
            jac_diag_stator,
            jac_off_rotor,
            jac_off_stator,
            source_rotor,
            source_stator,
            rotor_state,
            lists,
            face_count,
            margin_weight,
        )

    field = P(None, "span", None, "circ")
    matrix = P(None, None, "span", None, "circ")
    placed = (field,) * 4 + (matrix,) * 2 + (field,) * 2
    placed = placed + (
        P(None, "span", "circ"),
        P("span", None, None),
        P("span", None),
        P("span", None, None, None),
    )
    return jax.shard_map(
        per_device, mesh=mesh, in_specs=placed, out_specs=(field, field), check_vma=False
    )
```

```python
import functools

import jax
import jax.numpy as jnp
from jax import lax
from jax.experimental import pallas as pl
from jax.experimental.pallas import tpu as pltpu
from jax.sharding import PartitionSpec as P

STEPS = 2
STEP_SIZE = 0.1
COUPLING = 0.2
COARSE = 8
STRIDE = 8
OFFSET = 4
REACH = 6
SLOTS = 2 * REACH + 1
COMMON = 4
FILLED = REACH + COMMON
BESIDE = 3
HOMES = 2 * BESIDE + 1
SEEN = 7


def kernel(
    ring,
    band,
    adj_r,
    adj_s,
    diag_r,
    diag_s,
    off_r,
    off_s,
    src_r,
    src_s,
    rstate,
    margin,
    count,
    weight,
    out_r,
    out_s,
    adj,
    diag,
    off,
    src,
    wts,
    lists,
    live,
    pick,
    pad,
    part,
    adj1,
    edge,
    rows,
    home,
    home_f,
    near_a,
    near_b,
    near_f,
    sent_n,
    prim,
    face,
    flux,
    far_a0,
    far_a1,
    far_b0,
    far_b1,
    sent_f,
    sent_d,
    side,
    brow,
    qtab,
    ptab,
    dtab,
    wtab,
    pull,
    in_sem,
    out_sem,
    edge_sem,
    land_sem,
    send_sem,
    tip_sem,
):
    c = lax.axis_index("circ")
    s = lax.axis_index("span")
    blocks = 2 * ring

    def circ(shift):
        return {"circ": lax.rem(c + (shift + ring), ring)}

    def span(shift):
        return {"span": lax.rem(s + (shift + band), band)}

    def remote(source, target, sent, landed, where):
        return pltpu.make_async_remote_copy(
            src_ref=source,
            dst_ref=target,
            send_sem=sent,
            recv_sem=landed,
            device_id=where,
            device_id_type=pl.DeviceIdType.MESH,
        )

    barrier = pltpu.get_barrier_semaphore()

    def greet(where):
        pl.semaphore_signal(
            barrier, inc=1, device_id=where, device_id_type=pl.DeviceIdType.MESH
        )

    far = [x for x in range(OFFSET, ring, STRIDE) if REACH < x < ring - REACH]
    for shift in far + list(range(1, REACH + 1)) + list(range(-REACH, 0)):
        greet(circ(shift))
    greet(span(1))
    greet(span(-1))

    loads = [
        (adj_s, adj.at[1]),
        (adj_r, adj.at[0]),
        (margin, lists),
        (count, live),
        (off_s, off.at[1]),
        (diag_s, diag.at[1]),
        (src_s, src.at[1]),
        (off_r, off.at[0]),
        (diag_r, diag.at[0]),
        (src_r, src.at[0]),
        (rstate, pick),
        (weight, wts),
    ]
    copies = [pltpu.make_async_copy(a, b, in_sem.at[i]) for i, (a, b) in enumerate(loads)]
    for one in copies:
        one.start()

    def coarse(piece, landing, sign, n):
        @pl.loop(0, COARSE)
        def _(a):
            away = sign * (STRIDE * a + OFFSET)
            remote(piece, landing.at[a], send_sem.at[n], land_sem.at[n], circ(away)).start()

    def fine(piece, landing, sign, n):
        @pl.loop(1, REACH + 1)
        def _(t):
            remote(piece, landing.at[t], send_sem.at[n], land_sem.at[n], circ(sign * t)).start()
            low = landing.at[SLOTS - t]
            remote(piece, low, send_sem.at[n], land_sem.at[n], circ(-sign * t)).start()

    def fine_rows(piece, landing, n):
        def go(row, slot, away):
            source = piece if row is None else piece.at[row]
            target = landing.at[slot] if row is None else landing.at[slot, row]
            remote(source, target, send_sem.at[n], land_sem.at[n], circ(away)).start()

        @pl.loop(1, COMMON + 1)
        def _(t):
            go(None, t, t)
            go(None, SLOTS - t, -t)

        @pl.loop(COMMON + 1, REACH + 1)
        def _(t):
            go(1, t, t)
            go(0, SLOTS - t, -t)

    def drain(view, sem):
        pltpu.make_async_copy(view, view, sem).wait()

    def edges(source, step, field):
        lower = source.at[field, :, :, :, pl.ds(0, 128)]
        upper = source.at[field, :, :, :, pl.ds(128, 128)]
        sems = edge_sem.at[step, field]
        return [
            remote(upper, edge.at[step, 0, field], sems.at[4], sems.at[0], circ(1)),
            remote(lower, edge.at[step, 1, field], sems.at[5], sems.at[1], circ(-1)),
            remote(
                source.at[field, :, 1], rows.at[step, 0, field], sems.at[6], sems.at[2], span(1)
            ),
            remote(
                source.at[field, :, 0], rows.at[step, 1, field], sems.at[7], sems.at[3], span(-1)
            ),
        ]

    def begin(copies):
        for one in copies:
            one.start()
        return copies

    def finish(copies):
        for one in copies:
            one.wait()

    def front(target, source, row, half):
        target[row, :, half : half + 1, :] = source[1, :, row, 0:1, pl.ds(half * 128, 128)]

    pieces = [(row, half) for row in range(2) for half in range(2)]
    pad[...] = jnp.zeros_like(pad)
    qtab[...] = jnp.zeros_like(qtab)
    ptab[...] = jnp.zeros_like(ptab)
    dtab[...] = jnp.zeros_like(dtab)
    for landing in (far_b0, far_b1):
        for t in range(COMMON + 1, REACH + 1):
            landing[t, 0] = jnp.zeros_like(landing[t, 0])
            landing[SLOTS - t, 1] = jnp.zeros_like(landing[t, 0])
    wtab[...] = jnp.zeros_like(wtab)
    copies[0].wait()
    for row, half in pieces:
        front(sent_f.at[0], adj, row, half)
    copies[1].wait()
    pl.semaphore_wait(barrier, len(far) + 2 * REACH + 2)

    first = sent_f.at[0]
    tips = begin(
        [
            remote(first, side.at[0], tip_sem.at[4], tip_sem.at[0], circ(1)),
            remote(first, side.at[1], tip_sem.at[5], tip_sem.at[1], circ(-1)),
            remote(first.at[1], brow.at[0], tip_sem.at[6], tip_sem.at[2], span(1)),
            remote(first.at[0], brow.at[1], tip_sem.at[7], tip_sem.at[3], span(-1)),
        ]
    )
    coarse(first, far_a0, 1, 1)
    coarse(rstate, near_a, -1, 0)

    def local_part(x, field):
        pad[field, :, :, 1:5, :] = x[...]
        value = diag[field] * x[...] - src[field]
        value = value - COUPLING * (pad[field, :, :, 0:4, :] + pad[field, :, :, 2:6, :])

        def add(w, total):
            return total + off[field, w].astype(jnp.float32) * x[w][None]

        part[field] = lax.fori_loop(0, off.shape[1], add, value)

    lane = lax.broadcasted_iota(jnp.int32, (1, 1, 1, 128), 3)
    below = jnp.where(s == 0, 0.0, 1.0).astype(jnp.float32)
    above = jnp.where(s == band - 1, 0.0, 1.0).astype(jnp.float32)

    def advance(x, result, field, step):
        for half in range(2):
            here = pl.ds(half * 128, 128)
            other = pl.ds(128 - half * 128, 128)
            mine = x[:, :, :, here]
            before = edge[step, 0, field] if half == 0 else x[:, :, :, other]
            after = x[:, :, :, other] if half == 0 else edge[step, 1, field]
            left = pltpu.roll(jnp.where(lane == 127, before, mine), 1, axis=3)
            right = pltpu.roll(jnp.where(lane == 0, after, mine), 127, axis=3)
            beside = left + right
            spanwise0 = rows[step, 0, field, :, :, here] * below + x[:, 1, :, here]
            spanwise1 = rows[step, 1, field, :, :, here] * above + x[:, 0, :, here]
            whole = part[field, :, :, :, here] - COUPLING * beside
            result[:, 0, :, here] = mine[:, 0] - STEP_SIZE * (whole[:, 0] - COUPLING * spanwise0)
            result[:, 1, :, here] = mine[:, 1] - STEP_SIZE * (whole[:, 1] - COUPLING * spanwise1)

    for one in copies[4:7]:
        one.wait()
    local_part(adj.at[1], 1)
    finish(tips)
    line = lax.broadcasted_iota(jnp.int32, (1, 1, 128), 2)
    for row, half in pieces:

        def mine(row, half):
            return sent_f[0, row, :, half : half + 1, :]

        x = mine(row, half)
        before = side[0, row, :, 1:2, :] if half == 0 else mine(row, 0)
        after = mine(row, 1) if half == 0 else side[1, row, :, 0:1, :]
        around = pltpu.roll(jnp.where(line == 127, before, x), 1, axis=2)
        around = around + pltpu.roll(jnp.where(line == 0, after, x), 127, axis=2)
        outer = brow[row, :, half : half + 1, :] * (below if row == 0 else above)
        around = around + outer + mine(1 - row, half)
        value = part[1, :, row, 0:1, pl.ds(half * 128, 128)] - COUPLING * around
        sent_d[0, row, :, half : half + 1, :] = -STEP_SIZE * value
    coarse(sent_d.at[0], far_a1, 1, 2)

    @pl.loop(1, BESIDE + 1)
    def _(u):
        remote(rstate, home.at[u], send_sem.at[6], land_sem.at[6], circ(-u)).start()
        remote(rstate, home.at[HOMES - u], send_sem.at[6], land_sem.at[6], circ(u)).start()

    edges0_s = begin(edges(adj, 0, 1))
    edges0_r = begin(edges(adj, 0, 0))


    copies[2].wait()
    copies[3].wait()
    start = lists[0, 0, 0]

    def lowest(b, least):
        for row in range(2):
            e = ((lists[row, 0, b] - b - 4 * row - start + 2 + blocks) & (blocks - 1)) - 2
            least = jnp.minimum(least, e)
        return least

    base = (start + lax.fori_loop(0, blocks, lowest, jnp.int32(0), unroll=8) + blocks) & (blocks - 1)
    shift = lax.shift_right_logical(base, 1) + 3
    fine_at = ((shift - 1) & 7) - 3
    coarse_at = lax.shift_right_logical(shift - fine_at - OFFSET, 3) & 7

    for one in copies[7:]:
        one.wait()
    local_part(adj.at[0], 0)

    drain(far_a0, land_sem.at[1])
    chosen = far_a0[coarse_at]
    sent_f[1] = chosen
    far_b0[0] = chosen
    fine_rows(sent_f.at[1], far_b0, 4)
    drain(near_a, land_sem.at[0])
    chosen = near_a[coarse_at]
    sent_n[...] = chosen
    near_b[0] = chosen
    fine(sent_n, near_b, -1, 3)

    def wrap(t, size):
        t = t + (size & lax.shift_right_arithmetic(t, 31))
        return jnp.minimum(t, size - 1)

    def masked(factor, k, alive):
        shape = factor.shape
        return jnp.where(jnp.full(shape, k) < jnp.full(shape, alive), factor, 0.0)

    home[0] = pick[...]
    drain(home.at[pl.ds(1, HOMES - 1)], land_sem.at[6])
    for half in range(2):
        home_f[:, half] = home[:, :, :, pl.ds(half * 128, 128)].astype(jnp.float32)

    places = [(row, i) for row in range(2) for i in range(SEEN)]
    owners = []
    for row, i in places:
        b = (2 * c + 1 - base - 4 * row - i + 2 * blocks) & (blocks - 1)
        owners.append(b)
        first = lists[row, 0, b]
        alive = live[row, b]
        total = jnp.zeros((6, 1, 128), jnp.float32)
        for k in range(4):
            near = (first + k - 2 * c + 2 * BESIDE + blocks) & (blocks - 1)
            u = wrap(lax.shift_right_logical(near, 1) - BESIDE, HOMES)
            got = home_f[u, near & 1, :, row : row + 1, :]
            total = total + masked(wts[row, b, k : k + 1, :], k, alive)[None] * got
        qtab[row, :, i : i + 1, :] = total
        for block in range(2):
            if not 0 <= i - 1 + block < SEEN - 1:
                continue
            k = (2 * c + block - first + blocks) & (blocks - 1)
            factor = wts[row, b, pl.ds(jnp.minimum(k, 3), 1), :]
            wtab[row, block, i : i + 1, :] = masked(factor, k, alive)

    drain(far_a1, land_sem.at[2])
    chosen = far_a1[coarse_at]
    sent_d[1] = chosen
    far_b1[0] = chosen
    fine_rows(sent_d.at[1], far_b1, 5)

    finish(edges0_s)
    advance(adj.at[1], adj1.at[1], 1, 0)
    finish(edges0_r)
    advance(adj.at[0], adj1.at[0], 0, 0)

    def gather(landing, table):
        for (row, i), b in zip(places, owners):
            delta = (b - 2 * c + 2 * shift + 4 + blocks) & (blocks - 1)
            slot = wrap(fine_at - lax.shift_right_logical(delta, 1) + 2, SLOTS)
            table[row, :, i : i + 1, :] = landing[slot, row, :, pl.ds(delta & 1, 1), :]

    def speeds_of(q):
        return jnp.sqrt(1.0 + q * q)

    def interface_flux(q, p, axis):
        projection = jnp.sum(q * p, axis=axis, keepdims=True)
        projection = projection / (6.0 + jnp.sum(q * q, axis=axis, keepdims=True))
        return speeds_of(q) * p + 0.5 * q * projection

    def pulled(value):
        wire = value.astype(jnp.bfloat16).astype(jnp.float32)
        for row in range(2):
            for block in range(2):
                total = jnp.sum(wtab[row, block][None] * wire[row], axis=1, keepdims=True)
                pull[:, row : row + 1, pl.ds(block * 128, 128)] = total

    drain(far_b0.at[pl.ds(1, FILLED)], land_sem.at[4])
    gather(far_b0, ptab)
    first_flux = interface_flux(qtab[...], ptab[...], 1)
    pulled(first_flux)
    for row in range(2):
        adj1[0, :, row, 3:4, :] = adj1[0, :, row, 3:4, :] + STEP_SIZE * pull[:, row : row + 1, :]
    edges1_r = begin(edges(adj1, 1, 0))
    ptab[...] = ptab[...] - STEP_SIZE * first_flux

    drain(near_b.at[pl.ds(1, SLOTS - 1)], land_sem.at[3])
    for half in range(2):
        near_f[:, half] = near_b[:, :, :, pl.ds(half * 128, 128)].astype(jnp.float32)
    for row in range(2):
        for block in range(2):
            b = 2 * c + block
            first = lists[row, 0, b]
            alive = live[row, b]
            total = jnp.zeros((6, 1, 128), jnp.float32)
            for k in range(4):
                delta = (first + k - 2 * c - 2 * shift + 6 + 2 * blocks) & (blocks - 1)
                slot = wrap(fine_at + lax.shift_right_logical(delta, 1) - 3, SLOTS)
                got = near_f[slot, delta & 1, :, row : row + 1, :]
                total = total + masked(wts[row, b, k : k + 1, :], k, alive)[None] * got
            prim[:, row : row + 1, pl.ds(block * 128, 128)] = total
    for row in range(2):
        face[:, row : row + 1, :] = adj[1, :, row, 0:1, :]
    value = STEP_SIZE * interface_flux(prim[...], face[...], 0)
    flux[...] = value
    for row in range(2):
        moved = adj1[1, :, row, 0:1, :] - flux[:, row : row + 1, :]
        adj1[1, :, row, 0:1, :] = moved
        face[:, row : row + 1, :] = moved
    edges1_s = begin(edges(adj1, 1, 1))
    flux[...] = STEP_SIZE * interface_flux(prim[...], face[...], 0)

    local_part(adj1.at[0], 0)
    local_part(adj1.at[1], 1)

    finish(edges1_s)
    advance(adj1.at[1], adj.at[1], 1, 1)
    for row in range(2):
        adj[1, :, row, 0:1, :] = adj[1, :, row, 0:1, :] - flux[:, row : row + 1, :]
    store_s = pltpu.make_async_copy(adj.at[1], out_s, out_sem.at[0])
    store_s.start()

    finish(edges1_r)
    advance(adj1.at[0], adj.at[0], 0, 1)
    drain(far_b1.at[pl.ds(1, FILLED)], land_sem.at[5])
    gather(far_b1, dtab)
    pulled(interface_flux(qtab[...], ptab[...] + dtab[...], 1))
    for row in range(2):
        adj[0, :, row, 3:4, :] = adj[0, :, row, 3:4, :] + STEP_SIZE * pull[:, row : row + 1, :]
    store_r = pltpu.make_async_copy(adj.at[0], out_r, out_sem.at[1])
    store_r.start()

    drain(near_a, send_sem.at[0])
    drain(far_a0, send_sem.at[1])
    drain(far_a1, send_sem.at[2])
    drain(near_b.at[pl.ds(1, SLOTS - 1)], send_sem.at[3])
    drain(far_b0.at[pl.ds(1, FILLED)], send_sem.at[4])
    drain(far_b1.at[pl.ds(1, FILLED)], send_sem.at[5])
    drain(home.at[pl.ds(1, HOMES - 1)], send_sem.at[6])
    store_s.wait()
    store_r.wait()


def deliver(from_r, from_s, out_r, out_s, sem):
    moves = [
        pltpu.make_async_copy(from_r, out_r, sem.at[0]),
        pltpu.make_async_copy(from_s, out_s, sem.at[1]),
    ]
    for one in moves:
        one.start()
    for one in moves:
        one.wait()


def solution(mesh):
    ring, band = mesh.shape["circ"], mesh.shape["span"]

    def per_device(
        adjoint_rotor,
        adjoint_stator,
        jac_diag_rotor,
        jac_diag_stator,
        jac_off_rotor,
        jac_off_stator,
        source_rotor,
        source_stator,
        rotor_state,
        margin_block,
        face_count,
        margin_weight,
    ):
        f32, bf16 = jnp.float32, jnp.bfloat16
        shape = adjoint_rotor.shape
        piece = rotor_state.shape
        split = (2, 6, 2, 128)
        lists = jnp.transpose(margin_block, (0, 2, 1))
        out = jax.ShapeDtypeStruct(shape, f32)
        hbm = pl.BlockSpec(memory_space=pltpu.HBM)
        swept = pl.pallas_call(
            functools.partial(kernel, ring, band),
            out_shape=(out, out),
            in_specs=[hbm] * 12,
            out_specs=(hbm, hbm),
            scratch_shapes=[
                pltpu.VMEM((2,) + shape, f32),
                pltpu.VMEM((2,) + shape, f32),
                pltpu.VMEM((2,) + jac_off_rotor.shape, bf16),
                pltpu.VMEM((2,) + shape, f32),
                pltpu.VMEM(margin_weight.shape, f32),
                pltpu.SMEM(lists.shape, jnp.int32),
                pltpu.SMEM(face_count.shape, jnp.int32),
                pltpu.VMEM(piece, bf16),
                pltpu.VMEM((2, 6, 2, 8, 256), f32),
                pltpu.VMEM((2,) + shape, f32),
                pltpu.VMEM((2,) + shape, f32),
                pltpu.VMEM((STEPS, 2, 2, 6, 2, 4, 128), f32),
                pltpu.VMEM((STEPS, 2, 2, 6, 4, 256), f32),
                pltpu.VMEM((HOMES,) + piece, bf16),
                pltpu.VMEM((HOMES,) + split, f32),
                pltpu.VMEM((COARSE,) + piece, bf16),
                pltpu.VMEM((SLOTS,) + piece, bf16),
                pltpu.VMEM((SLOTS,) + split, f32),
                pltpu.VMEM(piece, bf16),
                pltpu.VMEM(piece, f32),
                pltpu.VMEM(piece, f32),
                pltpu.VMEM(piece, f32),
                pltpu.VMEM((COARSE,) + split, f32),
                pltpu.VMEM((COARSE,) + split, f32),
                pltpu.VMEM((SLOTS,) + split, f32),
                pltpu.VMEM((SLOTS,) + split, f32),
                pltpu.VMEM((2,) + split, f32),
                pltpu.VMEM((2,) + split, f32),
                pltpu.VMEM((2,) + split, f32),
                pltpu.VMEM((2,) + split[1:], f32),
                pltpu.VMEM((2, 6, 8, 128), f32),
                pltpu.VMEM((2, 6, 8, 128), f32),
                pltpu.VMEM((2, 6, 8, 128), f32),
                pltpu.VMEM((2, 2, 8, 128), f32),
                pltpu.VMEM(piece, f32),
                pltpu.SemaphoreType.DMA((12,)),
                pltpu.SemaphoreType.DMA((2,)),
                pltpu.SemaphoreType.DMA((STEPS, 2, 8)),
                pltpu.SemaphoreType.DMA((7,)),
                pltpu.SemaphoreType.DMA((7,)),
                pltpu.SemaphoreType.DMA((8,)),
            ],
            compiler_params=pltpu.CompilerParams(
                collective_id=0, has_side_effects=True, vmem_limit_bytes=60 * 1024 * 1024
            ),
            name="sweep",
        )(
            adjoint_rotor,
            adjoint_stator,
            jac_diag_rotor,
            jac_diag_stator,
            jac_off_rotor,
            jac_off_stator,
            source_rotor,
            source_stator,
            rotor_state,
            lists,
            face_count,
            margin_weight,
        )
        return pl.pallas_call(
            deliver,
            out_shape=(out, out),
            in_specs=[hbm] * 2,
            out_specs=(hbm, hbm),
            scratch_shapes=[pltpu.SemaphoreType.DMA((2,))],
            compiler_params=pltpu.CompilerParams(vmem_limit_bytes=60 * 1024 * 1024),
            name="deliver",
        )(*swept)

    field = P(None, "span", None, "circ")
    matrix = P(None, None, "span", None, "circ")
    placed = (field,) * 4 + (matrix,) * 2 + (field,) * 2
    placed = placed + (
        P(None, "span", "circ"),
        P("span", None, None),
        P("span", None),
        P("span", None, None, None),
    )
    return jax.shard_map(
        per_device, mesh=mesh, in_specs=placed, out_specs=(field, field), check_vma=False
    )
```

```python
import functools

import jax
import jax.numpy as jnp
from jax import lax
from jax.experimental import pallas as pl
from jax.experimental.pallas import tpu as pltpu
from jax.sharding import PartitionSpec as P

STEPS = 2
STEP_SIZE = 0.1
COUPLING = 0.2
COARSE = 8
STRIDE = 8
OFFSET = 4
REACH = 6
SLOTS = 2 * REACH + 1
COMMON = 4
FILLED = REACH + COMMON
BESIDE = 3
HOMES = 2 * BESIDE + 1
SEEN = 7


def kernel(
    ring,
    band,
    adj_r,
    adj_s,
    diag_r,
    diag_s,
    off_r,
    off_s,
    src_r,
    src_s,
    rstate,
    margin,
    count,
    weight,
    out_r,
    out_s,
    adj,
    diag,
    off,
    src,
    wts,
    lists,
    live,
    pick,
    pad,
    part,
    adj1,
    edge,
    rows,
    home,
    home_f,
    near_a,
    near_b,
    near_f,
    sent_n,
    prim,
    face,
    flux,
    far_a0,
    far_a1,
    far_b0,
    far_b1,
    sent_f,
    sent_d,
    side,
    brow,
    qtab,
    ptab,
    dtab,
    wtab,
    late,
    late_side,
    late_row,
    in_sem,
    out_sem,
    edge_sem,
    land_sem,
    send_sem,
    tip_sem,
    late_sem,
):
    c = lax.axis_index("circ")
    s = lax.axis_index("span")
    blocks = 2 * ring

    def circ(shift):
        return {"circ": lax.rem(c + (shift + ring), ring)}

    def span(shift):
        return {"span": lax.rem(s + (shift + band), band)}

    def remote(source, target, sent, landed, where):
        return pltpu.make_async_remote_copy(
            src_ref=source,
            dst_ref=target,
            send_sem=sent,
            recv_sem=landed,
            device_id=where,
            device_id_type=pl.DeviceIdType.MESH,
        )

    loads = [
        (adj_s, adj.at[1]),
        (adj_r, adj.at[0]),
        (margin, lists),
        (count, live),
        (off_s, off.at[1]),
        (diag_s, diag.at[1]),
        (src_s, src.at[1]),
        (off_r, off.at[0]),
        (diag_r, diag.at[0]),
        (src_r, src.at[0]),
        (rstate, pick),
        (weight, wts),
    ]
    copies = [pltpu.make_async_copy(a, b, in_sem.at[i]) for i, (a, b) in enumerate(loads)]
    copies[0].start()

    barrier = pltpu.get_barrier_semaphore()

    def greet(where):
        pl.semaphore_signal(
            barrier, inc=1, device_id=where, device_id_type=pl.DeviceIdType.MESH
        )

    far = [x for x in range(OFFSET, ring, STRIDE) if REACH < x < ring - REACH]
    for shift in far + list(range(1, REACH + 1)) + list(range(-REACH, 0)):
        greet(circ(shift))
    greet(span(1))
    greet(span(-1))

    for one in copies[1:]:
        one.start()

    def coarse(piece, landing, sign, n):
        for a in range(COARSE):
            away = sign * (STRIDE * a + OFFSET)
            remote(piece, landing.at[a], send_sem.at[n], land_sem.at[n], circ(away)).start()

    def fine(piece, landing, sign, n):
        for t in range(1, REACH + 1):
            remote(piece, landing.at[t], send_sem.at[n], land_sem.at[n], circ(sign * t)).start()
            low = landing.at[SLOTS - t]
            remote(piece, low, send_sem.at[n], land_sem.at[n], circ(-sign * t)).start()

    def fine_rows(piece, landing, n):
        def go(row, slot, away):
            source = piece if row is None else piece.at[row]
            target = landing.at[slot] if row is None else landing.at[slot, row]
            remote(source, target, send_sem.at[n], land_sem.at[n], circ(away)).start()

        for t in range(1, COMMON + 1):
            go(None, t, t)
            go(None, SLOTS - t, -t)

        for t in range(COMMON + 1, REACH + 1):
            go(1, t, t)
            go(0, SLOTS - t, -t)

    def drain(view, sem):
        pltpu.make_async_copy(view, view, sem).wait()

    def edges(source, step, field):
        lower = source.at[field, :, :, :, pl.ds(0, 128)]
        upper = source.at[field, :, :, :, pl.ds(128, 128)]
        sems = edge_sem.at[step, field]
        return [
            remote(upper, edge.at[step, 0, field], sems.at[4], sems.at[0], circ(1)),
            remote(lower, edge.at[step, 1, field], sems.at[5], sems.at[1], circ(-1)),
            remote(
                source.at[field, :, 1], rows.at[step, 0, field], sems.at[6], sems.at[2], span(1)
            ),
            remote(
                source.at[field, :, 0], rows.at[step, 1, field], sems.at[7], sems.at[3], span(-1)
            ),
        ]

    def begin(copies):
        for one in copies:
            one.start()
        return copies

    def finish(copies):
        for one in copies:
            one.wait()

    def front(target, source, row, half):
        target[row, :, half : half + 1, :] = source[1, :, row, 0:1, pl.ds(half * 128, 128)]

    pieces = [(row, half) for row in range(2) for half in range(2)]
    pad[...] = jnp.zeros_like(pad)
    qtab[...] = jnp.zeros_like(qtab)
    ptab[...] = jnp.zeros_like(ptab)
    dtab[...] = jnp.zeros_like(dtab)
    for landing in (far_b0, far_b1):
        for t in range(COMMON + 1, REACH + 1):
            landing[t, 0] = jnp.zeros_like(landing[t, 0])
            landing[SLOTS - t, 1] = jnp.zeros_like(landing[t, 0])
    wtab[...] = jnp.zeros_like(wtab)
    copies[0].wait()
    for row, half in pieces:
        front(sent_f.at[0], adj, row, half)
    copies[1].wait()
    pl.semaphore_wait(barrier, len(far) + 2 * REACH + 2)

    first = sent_f.at[0]
    tips = begin(
        [
            remote(first, side.at[0], tip_sem.at[4], tip_sem.at[0], circ(1)),
            remote(first, side.at[1], tip_sem.at[5], tip_sem.at[1], circ(-1)),
            remote(first.at[1], brow.at[0], tip_sem.at[6], tip_sem.at[2], span(1)),
            remote(first.at[0], brow.at[1], tip_sem.at[7], tip_sem.at[3], span(-1)),
        ]
    )
    coarse(first, far_a0, 1, 1)
    coarse(rstate, near_a, -1, 0)

    def local_part(x, field):
        pad[field, :, :, 1:5, :] = x[...]
        value = diag[field] * x[...] - src[field]
        value = value - COUPLING * (pad[field, :, :, 0:4, :] + pad[field, :, :, 2:6, :])

        def add(w, total):
            return total + off[field, w].astype(jnp.float32) * x[w][None]

        part[field] = lax.fori_loop(0, off.shape[1], add, value)

    lane = lax.broadcasted_iota(jnp.int32, (1, 1, 1, 128), 3)
    below = jnp.where(s == 0, 0.0, 1.0).astype(jnp.float32)
    above = jnp.where(s == band - 1, 0.0, 1.0).astype(jnp.float32)

    def advance(x, result, field, step):
        for half in range(2):
            here = pl.ds(half * 128, 128)
            other = pl.ds(128 - half * 128, 128)
            mine = x[:, :, :, here]
            before = edge[step, 0, field] if half == 0 else x[:, :, :, other]
            after = x[:, :, :, other] if half == 0 else edge[step, 1, field]
            left = pltpu.roll(jnp.where(lane == 127, before, mine), 1, axis=3)
            right = pltpu.roll(jnp.where(lane == 0, after, mine), 127, axis=3)
            beside = left + right
            spanwise0 = rows[step, 0, field, :, :, here] * below + x[:, 1, :, here]
            spanwise1 = rows[step, 1, field, :, :, here] * above + x[:, 0, :, here]
            whole = part[field, :, :, :, here] - COUPLING * beside
            result[:, 0, :, here] = mine[:, 0] - STEP_SIZE * (whole[:, 0] - COUPLING * spanwise0)
            result[:, 1, :, here] = mine[:, 1] - STEP_SIZE * (whole[:, 1] - COUPLING * spanwise1)

    for one in copies[4:7]:
        one.wait()
    local_part(adj.at[1], 1)
    finish(tips)
    line = lax.broadcasted_iota(jnp.int32, (1, 1, 128), 2)
    for row, half in pieces:

        def mine(row, half):
            return sent_f[0, row, :, half : half + 1, :]

        x = mine(row, half)
        before = side[0, row, :, 1:2, :] if half == 0 else mine(row, 0)
        after = mine(row, 1) if half == 0 else side[1, row, :, 0:1, :]
        around = pltpu.roll(jnp.where(line == 127, before, x), 1, axis=2)
        around = around + pltpu.roll(jnp.where(line == 0, after, x), 127, axis=2)
        outer = brow[row, :, half : half + 1, :] * (below if row == 0 else above)
        around = around + outer + mine(1 - row, half)
        value = part[1, :, row, 0:1, pl.ds(half * 128, 128)] - COUPLING * around
        sent_d[0, row, :, half : half + 1, :] = -STEP_SIZE * value
    coarse(sent_d.at[0], far_a1, 1, 2)

    for u in range(1, BESIDE + 1):
        remote(rstate, home.at[u], send_sem.at[6], land_sem.at[6], circ(-u)).start()
        remote(rstate, home.at[HOMES - u], send_sem.at[6], land_sem.at[6], circ(u)).start()

    edges0_s = begin(edges(adj, 0, 1))
    edges0_r = begin(edges(adj, 0, 0))


    copies[2].wait()
    copies[3].wait()
    start = lists[0, 0, 0]

    def lowest(b, least):
        for row in range(2):
            e = ((lists[row, 0, b] - b - 4 * row - start + 2 + blocks) & (blocks - 1)) - 2
            least = jnp.minimum(least, e)
        return least

    base = (start + lax.fori_loop(0, blocks, lowest, jnp.int32(0), unroll=8) + blocks) & (blocks - 1)
    shift = lax.shift_right_logical(base, 1) + 3
    fine_at = ((shift - 1) & 7) - 3
    coarse_at = lax.shift_right_logical(shift - fine_at - OFFSET, 3) & 7

    for one in copies[7:]:
        one.wait()
    local_part(adj.at[0], 0)

    drain(far_a0, land_sem.at[1])
    chosen = far_a0[coarse_at]
    sent_f[1] = chosen
    far_b0[0] = chosen
    fine_rows(sent_f.at[1], far_b0, 4)
    drain(near_a, land_sem.at[0])
    chosen = near_a[coarse_at]
    sent_n[...] = chosen
    near_b[0] = chosen
    fine(sent_n, near_b, -1, 3)

    def wrap(t, size):
        t = t + (size & lax.shift_right_arithmetic(t, 31))
        return jnp.minimum(t, size - 1)

    def masked(factor, k, alive):
        shape = factor.shape
        return jnp.where(jnp.full(shape, k) < jnp.full(shape, alive), factor, 0.0)

    home[0] = pick[...]
    drain(home.at[pl.ds(1, HOMES - 1)], land_sem.at[6])
    for half in range(2):
        home_f[:, half] = home[:, :, :, pl.ds(half * 128, 128)].astype(jnp.float32)

    places = [(row, i) for row in range(2) for i in range(SEEN)]
    owners = []
    for row, i in places:
        b = (2 * c + 1 - base - 4 * row - i + 2 * blocks) & (blocks - 1)
        owners.append(b)
        first = lists[row, 0, b]
        alive = live[row, b]
        total = jnp.zeros((6, 1, 128), jnp.float32)
        for k in range(4):
            near = (first + k - 2 * c + 2 * BESIDE + blocks) & (blocks - 1)
            u = wrap(lax.shift_right_logical(near, 1) - BESIDE, HOMES)
            got = home_f[u, near & 1, :, row : row + 1, :]
            total = total + masked(wts[row, b, k : k + 1, :], k, alive)[None] * got
        qtab[row, :, i : i + 1, :] = total
        for block in range(2):
            if not 0 <= i - 1 + block < SEEN - 1:
                continue
            k = (2 * c + block - first + blocks) & (blocks - 1)
            factor = wts[row, b, pl.ds(jnp.minimum(k, 3), 1), :]
            wtab[row, block, i : i + 1, :] = masked(factor, k, alive)

    drain(far_a1, land_sem.at[2])
    chosen = far_a1[coarse_at]
    sent_d[1] = chosen
    far_b1[0] = chosen
    fine_rows(sent_d.at[1], far_b1, 5)

    finish(edges0_s)
    advance(adj.at[1], adj1.at[1], 1, 0)
    finish(edges0_r)
    advance(adj.at[0], adj1.at[0], 0, 0)
    edges1_s = begin(edges(adj1, 1, 1))
    edges1_r = begin(edges(adj1, 1, 0))

    def gather(landing, table):
        for (row, i), b in zip(places, owners):
            delta = (b - 2 * c + 2 * shift + 4 + blocks) & (blocks - 1)
            slot = wrap(fine_at - lax.shift_right_logical(delta, 1) + 2, SLOTS)
            table[row, :, i : i + 1, :] = landing[slot, row, :, pl.ds(delta & 1, 1), :]

    def speeds_of(q):
        return jnp.sqrt(1.0 + q * q)

    def interface_flux(q, p, axis):
        projection = jnp.sum(q * p, axis=axis, keepdims=True)
        projection = projection / (6.0 + jnp.sum(q * q, axis=axis, keepdims=True))
        return speeds_of(q) * p + 0.5 * q * projection

    def pulled(value, which):
        wire = value.astype(jnp.bfloat16).astype(jnp.float32)
        for row in range(2):
            for block in range(2):
                total = jnp.sum(wtab[row, block][None] * wire[row], axis=1, keepdims=True)
                late[which, row, :, block : block + 1, :] = STEP_SIZE * total

    def corrections(field):
        piece, sems = late.at[field], late_sem.at[field]
        return [
            remote(piece, late_side.at[field, 0], sems.at[4], sems.at[0], circ(1)),
            remote(piece, late_side.at[field, 1], sems.at[5], sems.at[1], circ(-1)),
            remote(piece.at[1], late_row.at[field, 0], sems.at[6], sems.at[2], span(1)),
            remote(piece.at[0], late_row.at[field, 1], sems.at[7], sems.at[3], span(-1)),
        ]

    def correct(target, field, layer, which):
        for row, half in pieces:
            lanes = pl.ds(half * 128, 128)
            old = target[field, :, row, layer : layer + 1, lanes]
            new = old + late[which, row, :, half : half + 1, :]
            target[field, :, row, layer : layer + 1, lanes] = new

    def settle(early, late_copies, field, layer):
        for one in early:
            one.wait_recv()
        finish(late_copies)
        for row, end in pieces:
            old = edge[1, end, field, :, row, layer : layer + 1, :]
            new = old + late_side[field, end, row, :, 1 - end : 2 - end, :]
            edge[1, end, field, :, row, layer : layer + 1, :] = new
        for end, half in pieces:
            lanes = pl.ds(half * 128, 128)
            old = rows[1, end, field, :, layer : layer + 1, lanes]
            new = old + late_row[field, end, :, half : half + 1, :]
            rows[1, end, field, :, layer : layer + 1, lanes] = new

    drain(far_b0.at[pl.ds(1, FILLED)], land_sem.at[4])
    gather(far_b0, ptab)
    first_flux = interface_flux(qtab[...], ptab[...], 1)
    pulled(first_flux, 0)
    late_r = begin(corrections(0))
    for one in edges1_r:
        one.wait_send()
    correct(adj1, 0, 3, 0)
    ptab[...] = ptab[...] - STEP_SIZE * first_flux

    drain(near_b.at[pl.ds(1, SLOTS - 1)], land_sem.at[3])
    for half in range(2):
        near_f[:, half] = near_b[:, :, :, pl.ds(half * 128, 128)].astype(jnp.float32)
    for row in range(2):
        for block in range(2):
            b = 2 * c + block
            first = lists[row, 0, b]
            alive = live[row, b]
            total = jnp.zeros((6, 1, 128), jnp.float32)
            for k in range(4):
                delta = (first + k - 2 * c - 2 * shift + 6 + 2 * blocks) & (blocks - 1)
                slot = wrap(fine_at + lax.shift_right_logical(delta, 1) - 3, SLOTS)
                got = near_f[slot, delta & 1, :, row : row + 1, :]
                total = total + masked(wts[row, b, k : k + 1, :], k, alive)[None] * got
            prim[:, row : row + 1, pl.ds(block * 128, 128)] = total
    for row in range(2):
        face[:, row : row + 1, :] = adj[1, :, row, 0:1, :]
    value = STEP_SIZE * interface_flux(prim[...], face[...], 0)
    flux[...] = value
    for row, half in pieces:
        late[1, row, :, half : half + 1, :] = -flux[:, row : row + 1, pl.ds(half * 128, 128)]
    late_s = begin(corrections(1))
    for one in edges1_s:
        one.wait_send()
    for row in range(2):
        moved = adj1[1, :, row, 0:1, :] - flux[:, row : row + 1, :]
        adj1[1, :, row, 0:1, :] = moved
        face[:, row : row + 1, :] = moved
    flux[...] = STEP_SIZE * interface_flux(prim[...], face[...], 0)

    local_part(adj1.at[0], 0)
    local_part(adj1.at[1], 1)

    settle(edges1_s, late_s, 1, 0)
    advance(adj1.at[1], adj.at[1], 1, 1)
    for row in range(2):
        adj[1, :, row, 0:1, :] = adj[1, :, row, 0:1, :] - flux[:, row : row + 1, :]
    store_s = pltpu.make_async_copy(adj.at[1], out_s, out_sem.at[0])
    store_s.start()

    settle(edges1_r, late_r, 0, 3)
    advance(adj1.at[0], adj.at[0], 0, 1)
    drain(far_b1.at[pl.ds(1, FILLED)], land_sem.at[5])
    gather(far_b1, dtab)
    pulled(interface_flux(qtab[...], ptab[...] + dtab[...], 1), 2)
    correct(adj, 0, 3, 2)
    store_r = pltpu.make_async_copy(adj.at[0], out_r, out_sem.at[1])
    store_r.start()

    drain(near_a, send_sem.at[0])
    drain(far_a0, send_sem.at[1])
    drain(far_a1, send_sem.at[2])
    drain(near_b.at[pl.ds(1, SLOTS - 1)], send_sem.at[3])
    drain(far_b0.at[pl.ds(1, FILLED)], send_sem.at[4])
    drain(far_b1.at[pl.ds(1, FILLED)], send_sem.at[5])
    drain(home.at[pl.ds(1, HOMES - 1)], send_sem.at[6])
    store_s.wait()
    store_r.wait()


def deliver(from_r, from_s, out_r, out_s, held, sem):
    fetch = [
        pltpu.make_async_copy(from_r, held.at[0], sem.at[0]),
        pltpu.make_async_copy(from_s, held.at[1], sem.at[1]),
    ]
    store = [
        pltpu.make_async_copy(held.at[0], out_r, sem.at[2]),
        pltpu.make_async_copy(held.at[1], out_s, sem.at[3]),
    ]
    for one in fetch:
        one.start()
    for one, after in zip(fetch, store):
        one.wait()
        after.start()
    for one in store:
        one.wait()


def solution(mesh):
    ring, band = mesh.shape["circ"], mesh.shape["span"]

    def per_device(
        adjoint_rotor,
        adjoint_stator,
        jac_diag_rotor,
        jac_diag_stator,
        jac_off_rotor,
        jac_off_stator,
        source_rotor,
        source_stator,
        rotor_state,
        margin_block,
        face_count,
        margin_weight,
    ):
        f32, bf16 = jnp.float32, jnp.bfloat16
        shape = adjoint_rotor.shape
        piece = rotor_state.shape
        split = (2, 6, 2, 128)
        lists = jnp.transpose(margin_block, (0, 2, 1))
        out = jax.ShapeDtypeStruct(shape, f32)
        hbm = pl.BlockSpec(memory_space=pltpu.HBM)
        swept = pl.pallas_call(
            functools.partial(kernel, ring, band),
            out_shape=(out, out),
            in_specs=[hbm] * 12,
            out_specs=(hbm, hbm),
            scratch_shapes=[
                pltpu.VMEM((2,) + shape, f32),
                pltpu.VMEM((2,) + shape, f32),
                pltpu.VMEM((2,) + jac_off_rotor.shape, bf16),
                pltpu.VMEM((2,) + shape, f32),
                pltpu.VMEM(margin_weight.shape, f32),
                pltpu.SMEM(lists.shape, jnp.int32),
                pltpu.SMEM(face_count.shape, jnp.int32),
                pltpu.VMEM(piece, bf16),
                pltpu.VMEM((2, 6, 2, 8, 256), f32),
                pltpu.VMEM((2,) + shape, f32),
                pltpu.VMEM((2,) + shape, f32),
                pltpu.VMEM((STEPS, 2, 2, 6, 2, 4, 128), f32),
                pltpu.VMEM((STEPS, 2, 2, 6, 4, 256), f32),
                pltpu.VMEM((HOMES,) + piece, bf16),
                pltpu.VMEM((HOMES,) + split, f32),
                pltpu.VMEM((COARSE,) + piece, bf16),
                pltpu.VMEM((SLOTS,) + piece, bf16),
                pltpu.VMEM((SLOTS,) + split, f32),
                pltpu.VMEM(piece, bf16),
                pltpu.VMEM(piece, f32),
                pltpu.VMEM(piece, f32),
                pltpu.VMEM(piece, f32),
                pltpu.VMEM((COARSE,) + split, f32),
                pltpu.VMEM((COARSE,) + split, f32),
                pltpu.VMEM((SLOTS,) + split, f32),
                pltpu.VMEM((SLOTS,) + split, f32),
                pltpu.VMEM((2,) + split, f32),
                pltpu.VMEM((2,) + split, f32),
                pltpu.VMEM((2,) + split, f32),
                pltpu.VMEM((2,) + split[1:], f32),
                pltpu.VMEM((2, 6, 8, 128), f32),
                pltpu.VMEM((2, 6, 8, 128), f32),
                pltpu.VMEM((2, 6, 8, 128), f32),
                pltpu.VMEM((2, 2, 8, 128), f32),
                pltpu.VMEM((3,) + split, f32),
                pltpu.VMEM((2, 2) + split, f32),
                pltpu.VMEM((2, 2) + split[1:], f32),
                pltpu.SemaphoreType.DMA((12,)),
                pltpu.SemaphoreType.DMA((2,)),
                pltpu.SemaphoreType.DMA((STEPS, 2, 8)),
                pltpu.SemaphoreType.DMA((7,)),
                pltpu.SemaphoreType.DMA((7,)),
                pltpu.SemaphoreType.DMA((8,)),
                pltpu.SemaphoreType.DMA((2, 8)),
            ],
            compiler_params=pltpu.CompilerParams(
                collective_id=0, has_side_effects=True, vmem_limit_bytes=60 * 1024 * 1024
            ),
            name="sweep",
        )(
            adjoint_rotor,
            adjoint_stator,
            jac_diag_rotor,
            jac_diag_stator,
            jac_off_rotor,
            jac_off_stator,
            source_rotor,
            source_stator,
            rotor_state,
            lists,
            face_count,
            margin_weight,
        )
        return pl.pallas_call(
            deliver,
            out_shape=(out, out),
            in_specs=[hbm] * 2,
            out_specs=(hbm, hbm),
            scratch_shapes=[pltpu.VMEM((2,) + shape, f32), pltpu.SemaphoreType.DMA((4,))],
            compiler_params=pltpu.CompilerParams(vmem_limit_bytes=60 * 1024 * 1024),
            name="deliver",
        )(*swept)

    field = P(None, "span", None, "circ")
    matrix = P(None, None, "span", None, "circ")
    placed = (field,) * 4 + (matrix,) * 2 + (field,) * 2
    placed = placed + (
        P(None, "span", "circ"),
        P("span", None, None),
        P("span", None),
        P("span", None, None, None),
    )
    return jax.shard_map(
        per_device, mesh=mesh, in_specs=placed, out_specs=(field, field), check_vma=False
    )
```

```python
import functools

import jax
import jax.numpy as jnp
from jax import lax
from jax.experimental import pallas as pl
from jax.experimental.pallas import tpu as pltpu
from jax.sharding import PartitionSpec as P

STEPS = 2
STEP_SIZE = 0.1
COUPLING = 0.2
COARSE = 8
STRIDE = 8
OFFSET = 4
FAR_FIRST = (5, 6, 1, 2, 4, 7, 0, 3)
REACH = 6
SLOTS = 2 * REACH + 1
COMMON = 4
FILLED = REACH + COMMON
BESIDE = 3
HOMES = 2 * BESIDE + 1
SEEN = 7


def kernel(
    ring,
    band,
    adj_r,
    adj_s,
    diag_r,
    diag_s,
    off_r,
    off_s,
    src_r,
    src_s,
    rstate,
    margin,
    count,
    weight,
    out_r,
    out_s,
    adj,
    diag,
    off,
    src,
    wts,
    lists,
    live,
    pick,
    pad,
    part,
    adj1,
    edge,
    rows,
    home,
    home_f,
    near_a,
    near_b,
    near_f,
    sent_n,
    prim,
    face,
    flux,
    far_a0,
    far_a1,
    far_b0,
    far_b1,
    sent_f,
    sent_d,
    side,
    brow,
    qtab,
    ptab,
    dtab,
    wtab,
    late,
    late_side,
    late_row,
    in_sem,
    out_sem,
    edge_sem,
    land_sem,
    send_sem,
    tip_sem,
    late_sem,
):
    c = lax.axis_index("circ")
    s = lax.axis_index("span")
    blocks = 2 * ring

    def circ(shift):
        return {"circ": lax.rem(c + (shift + ring), ring)}

    def span(shift):
        return {"span": lax.rem(s + (shift + band), band)}

    def remote(source, target, sent, landed, where):
        return pltpu.make_async_remote_copy(
            src_ref=source,
            dst_ref=target,
            send_sem=sent,
            recv_sem=landed,
            device_id=where,
            device_id_type=pl.DeviceIdType.MESH,
        )

    loads = [
        (adj_s, adj.at[1]),
        (adj_r, adj.at[0]),
        (margin, lists),
        (count, live),
        (off_s, off.at[1]),
        (diag_s, diag.at[1]),
        (src_s, src.at[1]),
        (off_r, off.at[0]),
        (diag_r, diag.at[0]),
        (src_r, src.at[0]),
        (rstate, pick),
        (weight, wts),
    ]
    copies = [pltpu.make_async_copy(a, b, in_sem.at[i]) for i, (a, b) in enumerate(loads)]
    copies[0].start()

    barrier = pltpu.get_barrier_semaphore()

    def greet(where):
        pl.semaphore_signal(
            barrier, inc=1, device_id=where, device_id_type=pl.DeviceIdType.MESH
        )

    far = [STRIDE * a + OFFSET for a in FAR_FIRST]
    far = [x for x in far if REACH < x < ring - REACH]
    for shift in far + list(range(1, REACH + 1)) + list(range(-REACH, 0)):
        greet(circ(shift))
    greet(span(1))
    greet(span(-1))

    for one in copies[1:]:
        one.start()

    def coarse(piece, landing, sign, n):
        for a in FAR_FIRST:
            away = sign * (STRIDE * a + OFFSET)
            remote(piece, landing.at[a], send_sem.at[n], land_sem.at[n], circ(away)).start()

    def fine(piece, landing, sign, n):
        for t in range(REACH, 0, -1):
            remote(piece, landing.at[t], send_sem.at[n], land_sem.at[n], circ(sign * t)).start()
            low = landing.at[SLOTS - t]
            remote(piece, low, send_sem.at[n], land_sem.at[n], circ(-sign * t)).start()

    def fine_rows(piece, landing, n):
        def go(row, slot, away):
            source = piece if row is None else piece.at[row]
            target = landing.at[slot] if row is None else landing.at[slot, row]
            remote(source, target, send_sem.at[n], land_sem.at[n], circ(away)).start()

        for t in range(REACH, COMMON, -1):
            go(1, t, t)
            go(0, SLOTS - t, -t)

        for t in range(COMMON, 0, -1):
            go(None, t, t)
            go(None, SLOTS - t, -t)

    def drain(view, sem):
        pltpu.make_async_copy(view, view, sem).wait()

    def edges(source, step, field):
        lower = source.at[field, :, :, :, pl.ds(0, 128)]
        upper = source.at[field, :, :, :, pl.ds(128, 128)]
        sems = edge_sem.at[step, field]
        return [
            remote(upper, edge.at[step, 0, field], sems.at[4], sems.at[0], circ(1)),
            remote(lower, edge.at[step, 1, field], sems.at[5], sems.at[1], circ(-1)),
            remote(
                source.at[field, :, 1], rows.at[step, 0, field], sems.at[6], sems.at[2], span(1)
            ),
            remote(
                source.at[field, :, 0], rows.at[step, 1, field], sems.at[7], sems.at[3], span(-1)
            ),
        ]

    def begin(copies):
        for one in copies:
            one.start()
        return copies

    def finish(copies):
        for one in copies:
            one.wait()

    def front(target, source, row, half):
        target[row, :, half : half + 1, :] = source[1, :, row, 0:1, pl.ds(half * 128, 128)]

    pieces = [(row, half) for row in range(2) for half in range(2)]
    pad[...] = jnp.zeros_like(pad)
    qtab[...] = jnp.zeros_like(qtab)
    ptab[...] = jnp.zeros_like(ptab)
    dtab[...] = jnp.zeros_like(dtab)
    for landing in (far_b0, far_b1):
        for t in range(COMMON + 1, REACH + 1):
            landing[t, 0] = jnp.zeros_like(landing[t, 0])
            landing[SLOTS - t, 1] = jnp.zeros_like(landing[t, 0])
    wtab[...] = jnp.zeros_like(wtab)
    copies[0].wait()
    for row, half in pieces:
        front(sent_f.at[0], adj, row, half)
    copies[1].wait()
    pl.semaphore_wait(barrier, len(far) + 2 * REACH + 2)

    first = sent_f.at[0]
    tips = begin(
        [
            remote(first, side.at[0], tip_sem.at[4], tip_sem.at[0], circ(1)),
            remote(first, side.at[1], tip_sem.at[5], tip_sem.at[1], circ(-1)),
            remote(first.at[1], brow.at[0], tip_sem.at[6], tip_sem.at[2], span(1)),
            remote(first.at[0], brow.at[1], tip_sem.at[7], tip_sem.at[3], span(-1)),
        ]
    )
    coarse(first, far_a0, 1, 1)
    coarse(rstate, near_a, -1, 0)

    def local_part(x, field):
        pad[field, :, :, 1:5, :] = x[...]
        value = diag[field] * x[...] - src[field]
        value = value - COUPLING * (pad[field, :, :, 0:4, :] + pad[field, :, :, 2:6, :])

        def add(w, total):
            return total + off[field, w].astype(jnp.float32) * x[w][None]

        part[field] = lax.fori_loop(0, off.shape[1], add, value)

    lane = lax.broadcasted_iota(jnp.int32, (1, 1, 1, 128), 3)
    below = jnp.where(s == 0, 0.0, 1.0).astype(jnp.float32)
    above = jnp.where(s == band - 1, 0.0, 1.0).astype(jnp.float32)

    def advance(x, result, field, step):
        for half in range(2):
            here = pl.ds(half * 128, 128)
            other = pl.ds(128 - half * 128, 128)
            mine = x[:, :, :, here]
            before = edge[step, 0, field] if half == 0 else x[:, :, :, other]
            after = x[:, :, :, other] if half == 0 else edge[step, 1, field]
            left = pltpu.roll(jnp.where(lane == 127, before, mine), 1, axis=3)
            right = pltpu.roll(jnp.where(lane == 0, after, mine), 127, axis=3)
            beside = left + right
            spanwise0 = rows[step, 0, field, :, :, here] * below + x[:, 1, :, here]
            spanwise1 = rows[step, 1, field, :, :, here] * above + x[:, 0, :, here]
            whole = part[field, :, :, :, here] - COUPLING * beside
            result[:, 0, :, here] = mine[:, 0] - STEP_SIZE * (whole[:, 0] - COUPLING * spanwise0)
            result[:, 1, :, here] = mine[:, 1] - STEP_SIZE * (whole[:, 1] - COUPLING * spanwise1)

    for one in copies[4:7]:
        one.wait()
    local_part(adj.at[1], 1)
    finish(tips)
    line = lax.broadcasted_iota(jnp.int32, (1, 1, 128), 2)
    for row, half in pieces:

        def mine(row, half):
            return sent_f[0, row, :, half : half + 1, :]

        x = mine(row, half)
        before = side[0, row, :, 1:2, :] if half == 0 else mine(row, 0)
        after = mine(row, 1) if half == 0 else side[1, row, :, 0:1, :]
        around = pltpu.roll(jnp.where(line == 127, before, x), 1, axis=2)
        around = around + pltpu.roll(jnp.where(line == 0, after, x), 127, axis=2)
        outer = brow[row, :, half : half + 1, :] * (below if row == 0 else above)
        around = around + outer + mine(1 - row, half)
        value = part[1, :, row, 0:1, pl.ds(half * 128, 128)] - COUPLING * around
        sent_d[0, row, :, half : half + 1, :] = -STEP_SIZE * value
    coarse(sent_d.at[0], far_a1, 1, 2)

    for u in range(1, BESIDE + 1):
        remote(rstate, home.at[u], send_sem.at[6], land_sem.at[6], circ(-u)).start()
        remote(rstate, home.at[HOMES - u], send_sem.at[6], land_sem.at[6], circ(u)).start()

    edges0_s = begin(edges(adj, 0, 1))
    edges0_r = begin(edges(adj, 0, 0))


    copies[2].wait()
    copies[3].wait()
    start = lists[0, 0, 0]

    def lowest(b, least):
        for row in range(2):
            e = ((lists[row, 0, b] - b - 4 * row - start + 2 + blocks) & (blocks - 1)) - 2
            least = jnp.minimum(least, e)
        return least

    base = (start + lax.fori_loop(0, blocks, lowest, jnp.int32(0), unroll=8) + blocks) & (blocks - 1)
    shift = lax.shift_right_logical(base, 1) + 3
    fine_at = ((shift - 1) & 7) - 3
    coarse_at = lax.shift_right_logical(shift - fine_at - OFFSET, 3) & 7

    for one in copies[7:]:
        one.wait()
    local_part(adj.at[0], 0)

    drain(far_a0, land_sem.at[1])
    chosen = far_a0[coarse_at]
    sent_f[1] = chosen
    far_b0[0] = chosen
    fine_rows(sent_f.at[1], far_b0, 4)
    drain(near_a, land_sem.at[0])
    chosen = near_a[coarse_at]
    sent_n[...] = chosen
    near_b[0] = chosen
    fine(sent_n, near_b, -1, 3)

    def wrap(t, size):
        t = t + (size & lax.shift_right_arithmetic(t, 31))
        return jnp.minimum(t, size - 1)

    def masked(factor, k, alive):
        shape = factor.shape
        return jnp.where(jnp.full(shape, k) < jnp.full(shape, alive), factor, 0.0)

    home[0] = pick[...]
    drain(home.at[pl.ds(1, HOMES - 1)], land_sem.at[6])
    for half in range(2):
        home_f[:, half] = home[:, :, :, pl.ds(half * 128, 128)].astype(jnp.float32)

    places = [(row, i) for row in range(2) for i in range(SEEN)]
    owners = []
    for row, i in places:
        b = (2 * c + 1 - base - 4 * row - i + 2 * blocks) & (blocks - 1)
        owners.append(b)
        first = lists[row, 0, b]
        alive = live[row, b]
        total = jnp.zeros((6, 1, 128), jnp.float32)
        for k in range(4):
            near = (first + k - 2 * c + 2 * BESIDE + blocks) & (blocks - 1)
            u = wrap(lax.shift_right_logical(near, 1) - BESIDE, HOMES)
            got = home_f[u, near & 1, :, row : row + 1, :]
            total = total + masked(wts[row, b, k : k + 1, :], k, alive)[None] * got
        qtab[row, :, i : i + 1, :] = total
        for block in range(2):
            if not 0 <= i - 1 + block < SEEN - 1:
                continue
            k = (2 * c + block - first + blocks) & (blocks - 1)
            factor = wts[row, b, pl.ds(jnp.minimum(k, 3), 1), :]
            wtab[row, block, i : i + 1, :] = masked(factor, k, alive)

    drain(far_a1, land_sem.at[2])
    chosen = far_a1[coarse_at]
    sent_d[1] = chosen
    far_b1[0] = chosen
    fine_rows(sent_d.at[1], far_b1, 5)

    finish(edges0_s)
    advance(adj.at[1], adj1.at[1], 1, 0)
    finish(edges0_r)
    advance(adj.at[0], adj1.at[0], 0, 0)
    edges1_s = begin(edges(adj1, 1, 1))
    edges1_r = begin(edges(adj1, 1, 0))

    def gather(landing, table):
        for (row, i), b in zip(places, owners):
            delta = (b - 2 * c + 2 * shift + 4 + blocks) & (blocks - 1)
            slot = wrap(fine_at - lax.shift_right_logical(delta, 1) + 2, SLOTS)
            table[row, :, i : i + 1, :] = landing[slot, row, :, pl.ds(delta & 1, 1), :]

    def speeds_of(q):
        return jnp.sqrt(1.0 + q * q)

    def interface_flux(q, p, axis):
        projection = jnp.sum(q * p, axis=axis, keepdims=True)
        projection = projection / (6.0 + jnp.sum(q * q, axis=axis, keepdims=True))
        return speeds_of(q) * p + 0.5 * q * projection

    def pulled(value, which):
        wire = value.astype(jnp.bfloat16).astype(jnp.float32)
        for row in range(2):
            for block in range(2):
                total = jnp.sum(wtab[row, block][None] * wire[row], axis=1, keepdims=True)
                late[which, row, :, block : block + 1, :] = STEP_SIZE * total

    def corrections(field):
        piece, sems = late.at[field], late_sem.at[field]
        return [
            remote(piece, late_side.at[field, 0], sems.at[4], sems.at[0], circ(1)),
            remote(piece, late_side.at[field, 1], sems.at[5], sems.at[1], circ(-1)),
            remote(piece.at[1], late_row.at[field, 0], sems.at[6], sems.at[2], span(1)),
            remote(piece.at[0], late_row.at[field, 1], sems.at[7], sems.at[3], span(-1)),
        ]

    def correct(target, field, layer, which):
        for row, half in pieces:
            lanes = pl.ds(half * 128, 128)
            old = target[field, :, row, layer : layer + 1, lanes]
            new = old + late[which, row, :, half : half + 1, :]
            target[field, :, row, layer : layer + 1, lanes] = new

    def settle(early, late_copies, field, layer):
        for one in early:
            one.wait_recv()
        finish(late_copies)
        for row, end in pieces:
            old = edge[1, end, field, :, row, layer : layer + 1, :]
            new = old + late_side[field, end, row, :, 1 - end : 2 - end, :]
            edge[1, end, field, :, row, layer : layer + 1, :] = new
        for end, half in pieces:
            lanes = pl.ds(half * 128, 128)
            old = rows[1, end, field, :, layer : layer + 1, lanes]
            new = old + late_row[field, end, :, half : half + 1, :]
            rows[1, end, field, :, layer : layer + 1, lanes] = new

    drain(far_b0.at[pl.ds(1, FILLED)], land_sem.at[4])
    gather(far_b0, ptab)
    first_flux = interface_flux(qtab[...], ptab[...], 1)
    pulled(first_flux, 0)
    late_r = begin(corrections(0))
    for one in edges1_r:
        one.wait_send()
    correct(adj1, 0, 3, 0)
    ptab[...] = ptab[...] - STEP_SIZE * first_flux

    drain(near_b.at[pl.ds(1, SLOTS - 1)], land_sem.at[3])
    for half in range(2):
        near_f[:, half] = near_b[:, :, :, pl.ds(half * 128, 128)].astype(jnp.float32)
    for row in range(2):
        for block in range(2):
            b = 2 * c + block
            first = lists[row, 0, b]
            alive = live[row, b]
            total = jnp.zeros((6, 1, 128), jnp.float32)
            for k in range(4):
                delta = (first + k - 2 * c - 2 * shift + 6 + 2 * blocks) & (blocks - 1)
                slot = wrap(fine_at + lax.shift_right_logical(delta, 1) - 3, SLOTS)
                got = near_f[slot, delta & 1, :, row : row + 1, :]
                total = total + masked(wts[row, b, k : k + 1, :], k, alive)[None] * got
            prim[:, row : row + 1, pl.ds(block * 128, 128)] = total
    for row in range(2):
        face[:, row : row + 1, :] = adj[1, :, row, 0:1, :]
    value = STEP_SIZE * interface_flux(prim[...], face[...], 0)
    flux[...] = value
    for row, half in pieces:
        late[1, row, :, half : half + 1, :] = -flux[:, row : row + 1, pl.ds(half * 128, 128)]
    late_s = begin(corrections(1))
    for one in edges1_s:
        one.wait_send()
    for row in range(2):
        moved = adj1[1, :, row, 0:1, :] - flux[:, row : row + 1, :]
        adj1[1, :, row, 0:1, :] = moved
        face[:, row : row + 1, :] = moved
    flux[...] = STEP_SIZE * interface_flux(prim[...], face[...], 0)

    local_part(adj1.at[0], 0)
    local_part(adj1.at[1], 1)

    settle(edges1_s, late_s, 1, 0)
    advance(adj1.at[1], adj.at[1], 1, 1)
    for row in range(2):
        adj[1, :, row, 0:1, :] = adj[1, :, row, 0:1, :] - flux[:, row : row + 1, :]
    store_s = pltpu.make_async_copy(adj.at[1], out_s, out_sem.at[0])
    store_s.start()

    settle(edges1_r, late_r, 0, 3)
    advance(adj1.at[0], adj.at[0], 0, 1)
    drain(far_b1.at[pl.ds(1, FILLED)], land_sem.at[5])
    gather(far_b1, dtab)
    pulled(interface_flux(qtab[...], ptab[...] + dtab[...], 1), 2)
    correct(adj, 0, 3, 2)
    store_r = pltpu.make_async_copy(adj.at[0], out_r, out_sem.at[1])
    store_r.start()

    drain(near_a, send_sem.at[0])
    drain(far_a0, send_sem.at[1])
    drain(far_a1, send_sem.at[2])
    drain(near_b.at[pl.ds(1, SLOTS - 1)], send_sem.at[3])
    drain(far_b0.at[pl.ds(1, FILLED)], send_sem.at[4])
    drain(far_b1.at[pl.ds(1, FILLED)], send_sem.at[5])
    drain(home.at[pl.ds(1, HOMES - 1)], send_sem.at[6])
    store_s.wait()
    store_r.wait()


def deliver(from_r, from_s, out_r, out_s, held, sem):
    fetch = [
        pltpu.make_async_copy(from_r, held.at[0], sem.at[0]),
        pltpu.make_async_copy(from_s, held.at[1], sem.at[1]),
    ]
    store = [
        pltpu.make_async_copy(held.at[0], out_r, sem.at[2]),
        pltpu.make_async_copy(held.at[1], out_s, sem.at[3]),
    ]
    for one in fetch:
        one.start()
    for one, after in zip(fetch, store):
        one.wait()
        after.start()
    for one in store:
        one.wait()


def solution(mesh):
    ring, band = mesh.shape["circ"], mesh.shape["span"]

    def per_device(
        adjoint_rotor,
        adjoint_stator,
        jac_diag_rotor,
        jac_diag_stator,
        jac_off_rotor,
        jac_off_stator,
        source_rotor,
        source_stator,
        rotor_state,
        margin_block,
        face_count,
        margin_weight,
    ):
        f32, bf16 = jnp.float32, jnp.bfloat16
        shape = adjoint_rotor.shape
        piece = rotor_state.shape
        split = (2, 6, 2, 128)
        lists = jnp.transpose(margin_block, (0, 2, 1))
        out = jax.ShapeDtypeStruct(shape, f32)
        hbm = pl.BlockSpec(memory_space=pltpu.HBM)
        swept = pl.pallas_call(
            functools.partial(kernel, ring, band),
            out_shape=(out, out),
            in_specs=[hbm] * 12,
            out_specs=(hbm, hbm),
            scratch_shapes=[
                pltpu.VMEM((2,) + shape, f32),
                pltpu.VMEM((2,) + shape, f32),
                pltpu.VMEM((2,) + jac_off_rotor.shape, bf16),
                pltpu.VMEM((2,) + shape, f32),
                pltpu.VMEM(margin_weight.shape, f32),
                pltpu.SMEM(lists.shape, jnp.int32),
                pltpu.SMEM(face_count.shape, jnp.int32),
                pltpu.VMEM(piece, bf16),
                pltpu.VMEM((2, 6, 2, 8, 256), f32),
                pltpu.VMEM((2,) + shape, f32),
                pltpu.VMEM((2,) + shape, f32),
                pltpu.VMEM((STEPS, 2, 2, 6, 2, 4, 128), f32),
                pltpu.VMEM((STEPS, 2, 2, 6, 4, 256), f32),
                pltpu.VMEM((HOMES,) + piece, bf16),
                pltpu.VMEM((HOMES,) + split, f32),
                pltpu.VMEM((COARSE,) + piece, bf16),
                pltpu.VMEM((SLOTS,) + piece, bf16),
                pltpu.VMEM((SLOTS,) + split, f32),
                pltpu.VMEM(piece, bf16),
                pltpu.VMEM(piece, f32),
                pltpu.VMEM(piece, f32),
                pltpu.VMEM(piece, f32),
                pltpu.VMEM((COARSE,) + split, f32),
                pltpu.VMEM((COARSE,) + split, f32),
                pltpu.VMEM((SLOTS,) + split, f32),
                pltpu.VMEM((SLOTS,) + split, f32),
                pltpu.VMEM((2,) + split, f32),
                pltpu.VMEM((2,) + split, f32),
                pltpu.VMEM((2,) + split, f32),
                pltpu.VMEM((2,) + split[1:], f32),
                pltpu.VMEM((2, 6, 8, 128), f32),
                pltpu.VMEM((2, 6, 8, 128), f32),
                pltpu.VMEM((2, 6, 8, 128), f32),
                pltpu.VMEM((2, 2, 8, 128), f32),
                pltpu.VMEM((3,) + split, f32),
                pltpu.VMEM((2, 2) + split, f32),
                pltpu.VMEM((2, 2) + split[1:], f32),
                pltpu.SemaphoreType.DMA((12,)),
                pltpu.SemaphoreType.DMA((2,)),
                pltpu.SemaphoreType.DMA((STEPS, 2, 8)),
                pltpu.SemaphoreType.DMA((7,)),
                pltpu.SemaphoreType.DMA((7,)),
                pltpu.SemaphoreType.DMA((8,)),
                pltpu.SemaphoreType.DMA((2, 8)),
            ],
            compiler_params=pltpu.CompilerParams(
                collective_id=0, has_side_effects=True, vmem_limit_bytes=60 * 1024 * 1024
            ),
            name="sweep",
        )(
            adjoint_rotor,
            adjoint_stator,
            jac_diag_rotor,
            jac_diag_stator,
            jac_off_rotor,
            jac_off_stator,
            source_rotor,
            source_stator,
            rotor_state,
            lists,
            face_count,
            margin_weight,
        )
        return pl.pallas_call(
            deliver,
            out_shape=(out, out),
            in_specs=[hbm] * 2,
            out_specs=(hbm, hbm),
            scratch_shapes=[pltpu.VMEM((2,) + shape, f32), pltpu.SemaphoreType.DMA((4,))],
            compiler_params=pltpu.CompilerParams(vmem_limit_bytes=60 * 1024 * 1024),
            name="deliver",
        )(*swept)

    field = P(None, "span", None, "circ")
    matrix = P(None, None, "span", None, "circ")
    placed = (field,) * 4 + (matrix,) * 2 + (field,) * 2
    placed = placed + (
        P(None, "span", "circ"),
        P("span", None, None),
        P("span", None),
        P("span", None, None, None),
    )
    return jax.shard_map(
        per_device, mesh=mesh, in_specs=placed, out_specs=(field, field), check_vma=False
    )
```

```python
import functools

import jax
import jax.numpy as jnp
from jax import lax
from jax.experimental import pallas as pl
from jax.experimental.pallas import tpu as pltpu
from jax.sharding import PartitionSpec as P

STEPS = 2
STEP_SIZE = 0.1
COUPLING = 0.2
COARSE = 8
STRIDE = 8
OFFSET = 4
FAR_FIRST = (5, 6, 1, 2, 4, 7, 0, 3)
REACH = 6
SLOTS = 2 * REACH + 1
COMMON = 4
FILLED = REACH + COMMON
BESIDE = 3
HOMES = 2 * BESIDE + 1
SEEN = 7


def kernel(
    ring,
    band,
    adj_r,
    adj_s,
    diag_r,
    diag_s,
    off_r,
    off_s,
    src_r,
    src_s,
    rstate,
    margin,
    count,
    weight,
    out_r,
    out_s,
    adj,
    diag,
    off,
    src,
    wts,
    lists,
    live,
    pick,
    pad,
    part,
    adj1,
    edge,
    rows,
    home,
    home_f,
    near_a,
    near_b,
    near_f,
    sent_n,
    prim,
    face,
    flux,
    far_a0,
    far_a1,
    far_b0,
    far_b1,
    sent_f,
    sent_d,
    side,
    brow,
    qtab,
    ptab,
    dtab,
    wtab,
    late,
    late_side,
    late_row,
    in_sem,
    out_sem,
    edge_sem,
    land_sem,
    send_sem,
    tip_sem,
    late_sem,
):
    c = lax.axis_index("circ")
    s = lax.axis_index("span")
    blocks = 2 * ring

    def circ(shift):
        return {"circ": lax.rem(c + (shift + ring), ring)}

    def span(shift):
        return {"span": lax.rem(s + (shift + band), band)}

    def remote(source, target, sent, landed, where):
        return pltpu.make_async_remote_copy(
            src_ref=source,
            dst_ref=target,
            send_sem=sent,
            recv_sem=landed,
            device_id=where,
            device_id_type=pl.DeviceIdType.MESH,
        )

    loads = [
        (adj_s, adj.at[1]),
        (adj_r, adj.at[0]),
        (margin, lists),
        (count, live),
        (off_s, off.at[1]),
        (diag_s, diag.at[1]),
        (src_s, src.at[1]),
        (off_r, off.at[0]),
        (diag_r, diag.at[0]),
        (src_r, src.at[0]),
        (rstate, pick),
        (weight, wts),
    ]
    copies = [pltpu.make_async_copy(a, b, in_sem.at[i]) for i, (a, b) in enumerate(loads)]
    copies[0].start()

    barrier = pltpu.get_barrier_semaphore()

    def greet(where):
        pl.semaphore_signal(
            barrier, inc=1, device_id=where, device_id_type=pl.DeviceIdType.MESH
        )

    far = [STRIDE * a + OFFSET for a in FAR_FIRST]
    far = [x for x in far if REACH < x < ring - REACH]
    for shift in far + list(range(1, REACH + 1)) + list(range(-REACH, 0)):
        greet(circ(shift))
    greet(span(1))
    greet(span(-1))

    for one in copies[1:]:
        one.start()

    def coarse(piece, landing, sign, n):
        for a in FAR_FIRST:
            away = sign * (STRIDE * a + OFFSET)
            remote(piece, landing.at[a], send_sem.at[n], land_sem.at[n], circ(away)).start()

    def fine(piece, landing, sign, n):
        for t in range(REACH, 0, -1):
            remote(piece, landing.at[t], send_sem.at[n], land_sem.at[n], circ(sign * t)).start()
            low = landing.at[SLOTS - t]
            remote(piece, low, send_sem.at[n], land_sem.at[n], circ(-sign * t)).start()

    def fine_rows(piece, landing, n):
        def go(row, slot, away):
            source = piece if row is None else piece.at[row]
            target = landing.at[slot] if row is None else landing.at[slot, row]
            remote(source, target, send_sem.at[n], land_sem.at[n], circ(away)).start()

        for t in range(REACH, COMMON, -1):
            go(1, t, t)
            go(0, SLOTS - t, -t)

        for t in range(COMMON, 0, -1):
            go(None, t, t)
            go(None, SLOTS - t, -t)

    def drain(view, sem):
        pltpu.make_async_copy(view, view, sem).wait()

    def edges(source, step, field):
        lower = source.at[field, :, :, :, pl.ds(0, 128)]
        upper = source.at[field, :, :, :, pl.ds(128, 128)]
        sems = edge_sem.at[step, field]
        return [
            remote(upper, edge.at[step, 0, field], sems.at[4], sems.at[0], circ(1)),
            remote(lower, edge.at[step, 1, field], sems.at[5], sems.at[1], circ(-1)),
            remote(
                source.at[field, :, 1], rows.at[step, 0, field], sems.at[6], sems.at[2], span(1)
            ),
            remote(
                source.at[field, :, 0], rows.at[step, 1, field], sems.at[7], sems.at[3], span(-1)
            ),
        ]

    def begin(copies):
        for one in copies:
            one.start()
        return copies

    def finish(copies):
        for one in copies:
            one.wait()

    def front(target, source, row, half):
        target[row, :, half : half + 1, :] = source[1, :, row, 0:1, pl.ds(half * 128, 128)]

    pieces = [(row, half) for row in range(2) for half in range(2)]
    pad[...] = jnp.zeros_like(pad)
    qtab[...] = jnp.zeros_like(qtab)
    ptab[...] = jnp.zeros_like(ptab)
    dtab[...] = jnp.zeros_like(dtab)
    for landing in (far_b0, far_b1):
        for t in range(COMMON + 1, REACH + 1):
            landing[t, 0] = jnp.zeros_like(landing[t, 0])
            landing[SLOTS - t, 1] = jnp.zeros_like(landing[t, 0])
    wtab[...] = jnp.zeros_like(wtab)
    copies[0].wait()
    for row, half in pieces:
        front(sent_f.at[0], adj, row, half)
    copies[1].wait()
    pl.semaphore_wait(barrier, len(far) + 2 * REACH + 2)

    first = sent_f.at[0]
    tips = begin(
        [
            remote(first, side.at[0], tip_sem.at[4], tip_sem.at[0], circ(1)),
            remote(first, side.at[1], tip_sem.at[5], tip_sem.at[1], circ(-1)),
            remote(first.at[1], brow.at[0], tip_sem.at[6], tip_sem.at[2], span(1)),
            remote(first.at[0], brow.at[1], tip_sem.at[7], tip_sem.at[3], span(-1)),
        ]
    )
    coarse(first, far_a0, 1, 1)
    coarse(rstate, near_a, -1, 0)

    def local_part(x, field):
        pad[field, :, :, 1:5, :] = x[...]
        value = diag[field] * x[...] - src[field]
        value = value - COUPLING * (pad[field, :, :, 0:4, :] + pad[field, :, :, 2:6, :])

        def add(w, total):
            return total + off[field, w].astype(jnp.float32) * x[w][None]

        part[field] = lax.fori_loop(0, off.shape[1], add, value)

    lane = lax.broadcasted_iota(jnp.int32, (1, 1, 1, 128), 3)
    below = jnp.where(s == 0, 0.0, 1.0).astype(jnp.float32)
    above = jnp.where(s == band - 1, 0.0, 1.0).astype(jnp.float32)

    def advance(x, result, field, step):
        for half in range(2):
            here = pl.ds(half * 128, 128)
            other = pl.ds(128 - half * 128, 128)
            mine = x[:, :, :, here]
            before = edge[step, 0, field] if half == 0 else x[:, :, :, other]
            after = x[:, :, :, other] if half == 0 else edge[step, 1, field]
            left = pltpu.roll(jnp.where(lane == 127, before, mine), 1, axis=3)
            right = pltpu.roll(jnp.where(lane == 0, after, mine), 127, axis=3)
            beside = left + right
            spanwise0 = rows[step, 0, field, :, :, here] * below + x[:, 1, :, here]
            spanwise1 = rows[step, 1, field, :, :, here] * above + x[:, 0, :, here]
            whole = part[field, :, :, :, here] - COUPLING * beside
            result[:, 0, :, here] = mine[:, 0] - STEP_SIZE * (whole[:, 0] - COUPLING * spanwise0)
            result[:, 1, :, here] = mine[:, 1] - STEP_SIZE * (whole[:, 1] - COUPLING * spanwise1)

    for one in copies[4:7]:
        one.wait()
    local_part(adj.at[1], 1)
    finish(tips)
    line = lax.broadcasted_iota(jnp.int32, (1, 1, 128), 2)
    for row, half in pieces:

        def mine(row, half):
            return sent_f[0, row, :, half : half + 1, :]

        x = mine(row, half)
        before = side[0, row, :, 1:2, :] if half == 0 else mine(row, 0)
        after = mine(row, 1) if half == 0 else side[1, row, :, 0:1, :]
        around = pltpu.roll(jnp.where(line == 127, before, x), 1, axis=2)
        around = around + pltpu.roll(jnp.where(line == 0, after, x), 127, axis=2)
        outer = brow[row, :, half : half + 1, :] * (below if row == 0 else above)
        around = around + outer + mine(1 - row, half)
        value = part[1, :, row, 0:1, pl.ds(half * 128, 128)] - COUPLING * around
        sent_d[0, row, :, half : half + 1, :] = -STEP_SIZE * value
    coarse(sent_d.at[0], far_a1, 1, 2)

    for u in range(1, BESIDE + 1):
        remote(rstate, home.at[u], send_sem.at[6], land_sem.at[6], circ(-u)).start()
        remote(rstate, home.at[HOMES - u], send_sem.at[6], land_sem.at[6], circ(u)).start()


    copies[2].wait()
    copies[3].wait()
    start = lists[0, 0, 0]

    def lowest(b, least):
        for row in range(2):
            e = ((lists[row, 0, b] - b - 4 * row - start + 2 + blocks) & (blocks - 1)) - 2
            least = jnp.minimum(least, e)
        return least

    base = (start + lax.fori_loop(0, blocks, lowest, jnp.int32(0), unroll=8) + blocks) & (blocks - 1)
    shift = lax.shift_right_logical(base, 1) + 3
    fine_at = ((shift - 1) & 7) - 3
    coarse_at = lax.shift_right_logical(shift - fine_at - OFFSET, 3) & 7

    for one in copies[7:]:
        one.wait()
    local_part(adj.at[0], 0)

    drain(far_a0, land_sem.at[1])
    chosen = far_a0[coarse_at]
    sent_f[1] = chosen
    far_b0[0] = chosen
    fine_rows(sent_f.at[1], far_b0, 4)
    drain(near_a, land_sem.at[0])
    chosen = near_a[coarse_at]
    sent_n[...] = chosen
    near_b[0] = chosen
    fine(sent_n, near_b, -1, 3)
    edges0_s = begin(edges(adj, 0, 1))
    edges0_r = begin(edges(adj, 0, 0))

    def wrap(t, size):
        t = t + (size & lax.shift_right_arithmetic(t, 31))
        return jnp.minimum(t, size - 1)

    def masked(factor, k, alive):
        shape = factor.shape
        return jnp.where(jnp.full(shape, k) < jnp.full(shape, alive), factor, 0.0)

    home[0] = pick[...]
    drain(home.at[pl.ds(1, HOMES - 1)], land_sem.at[6])
    for half in range(2):
        home_f[:, half] = home[:, :, :, pl.ds(half * 128, 128)].astype(jnp.float32)

    places = [(row, i) for row in range(2) for i in range(SEEN)]
    owners = []
    for row, i in places:
        b = (2 * c + 1 - base - 4 * row - i + 2 * blocks) & (blocks - 1)
        owners.append(b)
        first = lists[row, 0, b]
        alive = live[row, b]
        total = jnp.zeros((6, 1, 128), jnp.float32)
        for k in range(4):
            near = (first + k - 2 * c + 2 * BESIDE + blocks) & (blocks - 1)
            u = wrap(lax.shift_right_logical(near, 1) - BESIDE, HOMES)
            got = home_f[u, near & 1, :, row : row + 1, :]
            total = total + masked(wts[row, b, k : k + 1, :], k, alive)[None] * got
        qtab[row, :, i : i + 1, :] = total
        for block in range(2):
            if not 0 <= i - 1 + block < SEEN - 1:
                continue
            k = (2 * c + block - first + blocks) & (blocks - 1)
            factor = wts[row, b, pl.ds(jnp.minimum(k, 3), 1), :]
            wtab[row, block, i : i + 1, :] = masked(factor, k, alive)

    drain(far_a1, land_sem.at[2])
    chosen = far_a1[coarse_at]
    sent_d[1] = chosen
    far_b1[0] = chosen
    fine_rows(sent_d.at[1], far_b1, 5)

    finish(edges0_s)
    advance(adj.at[1], adj1.at[1], 1, 0)
    finish(edges0_r)
    advance(adj.at[0], adj1.at[0], 0, 0)
    edges1_s = begin(edges(adj1, 1, 1))
    edges1_r = begin(edges(adj1, 1, 0))

    def gather(landing, table):
        for (row, i), b in zip(places, owners):
            delta = (b - 2 * c + 2 * shift + 4 + blocks) & (blocks - 1)
            slot = wrap(fine_at - lax.shift_right_logical(delta, 1) + 2, SLOTS)
            table[row, :, i : i + 1, :] = landing[slot, row, :, pl.ds(delta & 1, 1), :]

    def speeds_of(q):
        return jnp.sqrt(1.0 + q * q)

    def interface_flux(q, p, axis):
        projection = jnp.sum(q * p, axis=axis, keepdims=True)
        projection = projection / (6.0 + jnp.sum(q * q, axis=axis, keepdims=True))
        return speeds_of(q) * p + 0.5 * q * projection

    def pulled(value, which):
        wire = value.astype(jnp.bfloat16).astype(jnp.float32)
        for row in range(2):
            for block in range(2):
                total = jnp.sum(wtab[row, block][None] * wire[row], axis=1, keepdims=True)
                late[which, row, :, block : block + 1, :] = STEP_SIZE * total

    def corrections(field):
        piece, sems = late.at[field], late_sem.at[field]
        return [
            remote(piece, late_side.at[field, 0], sems.at[4], sems.at[0], circ(1)),
            remote(piece, late_side.at[field, 1], sems.at[5], sems.at[1], circ(-1)),
            remote(piece.at[1], late_row.at[field, 0], sems.at[6], sems.at[2], span(1)),
            remote(piece.at[0], late_row.at[field, 1], sems.at[7], sems.at[3], span(-1)),
        ]

    def correct(target, field, layer, which):
        for row, half in pieces:
            lanes = pl.ds(half * 128, 128)
            old = target[field, :, row, layer : layer + 1, lanes]
            new = old + late[which, row, :, half : half + 1, :]
            target[field, :, row, layer : layer + 1, lanes] = new

    def settle(early, late_copies, field, layer):
        for one in early:
            one.wait_recv()
        finish(late_copies)
        for row, end in pieces:
            old = edge[1, end, field, :, row, layer : layer + 1, :]
            new = old + late_side[field, end, row, :, 1 - end : 2 - end, :]
            edge[1, end, field, :, row, layer : layer + 1, :] = new
        for end, half in pieces:
            lanes = pl.ds(half * 128, 128)
            old = rows[1, end, field, :, layer : layer + 1, lanes]
            new = old + late_row[field, end, :, half : half + 1, :]
            rows[1, end, field, :, layer : layer + 1, lanes] = new

    drain(far_b0.at[pl.ds(1, FILLED)], land_sem.at[4])
    gather(far_b0, ptab)
    first_flux = interface_flux(qtab[...], ptab[...], 1)
    pulled(first_flux, 0)
    late_r = begin(corrections(0))
    for one in edges1_r:
        one.wait_send()
    correct(adj1, 0, 3, 0)
    ptab[...] = ptab[...] - STEP_SIZE * first_flux

    drain(near_b.at[pl.ds(1, SLOTS - 1)], land_sem.at[3])
    for half in range(2):
        near_f[:, half] = near_b[:, :, :, pl.ds(half * 128, 128)].astype(jnp.float32)
    for row in range(2):
        for block in range(2):
            b = 2 * c + block
            first = lists[row, 0, b]
            alive = live[row, b]
            total = jnp.zeros((6, 1, 128), jnp.float32)
            for k in range(4):
                delta = (first + k - 2 * c - 2 * shift + 6 + 2 * blocks) & (blocks - 1)
                slot = wrap(fine_at + lax.shift_right_logical(delta, 1) - 3, SLOTS)
                got = near_f[slot, delta & 1, :, row : row + 1, :]
                total = total + masked(wts[row, b, k : k + 1, :], k, alive)[None] * got
            prim[:, row : row + 1, pl.ds(block * 128, 128)] = total
    for row in range(2):
        face[:, row : row + 1, :] = adj[1, :, row, 0:1, :]
    value = STEP_SIZE * interface_flux(prim[...], face[...], 0)
    flux[...] = value
    for row, half in pieces:
        late[1, row, :, half : half + 1, :] = -flux[:, row : row + 1, pl.ds(half * 128, 128)]
    late_s = begin(corrections(1))
    for one in edges1_s:
        one.wait_send()
    for row in range(2):
        moved = adj1[1, :, row, 0:1, :] - flux[:, row : row + 1, :]
        adj1[1, :, row, 0:1, :] = moved
        face[:, row : row + 1, :] = moved
    flux[...] = STEP_SIZE * interface_flux(prim[...], face[...], 0)

    local_part(adj1.at[0], 0)
    local_part(adj1.at[1], 1)

    settle(edges1_s, late_s, 1, 0)
    advance(adj1.at[1], adj.at[1], 1, 1)
    for row in range(2):
        adj[1, :, row, 0:1, :] = adj[1, :, row, 0:1, :] - flux[:, row : row + 1, :]
    store_s = pltpu.make_async_copy(adj.at[1], out_s, out_sem.at[0])
    store_s.start()

    settle(edges1_r, late_r, 0, 3)
    advance(adj1.at[0], adj.at[0], 0, 1)
    drain(far_b1.at[pl.ds(1, FILLED)], land_sem.at[5])
    gather(far_b1, dtab)
    pulled(interface_flux(qtab[...], ptab[...] + dtab[...], 1), 2)
    correct(adj, 0, 3, 2)
    store_r = pltpu.make_async_copy(adj.at[0], out_r, out_sem.at[1])
    store_r.start()

    drain(near_a, send_sem.at[0])
    drain(far_a0, send_sem.at[1])
    drain(far_a1, send_sem.at[2])
    drain(near_b.at[pl.ds(1, SLOTS - 1)], send_sem.at[3])
    drain(far_b0.at[pl.ds(1, FILLED)], send_sem.at[4])
    drain(far_b1.at[pl.ds(1, FILLED)], send_sem.at[5])
    drain(home.at[pl.ds(1, HOMES - 1)], send_sem.at[6])
    store_s.wait()
    store_r.wait()


def deliver(from_r, from_s, out_r, out_s, held, sem):
    fetch = [
        pltpu.make_async_copy(from_r, held.at[0], sem.at[0]),
        pltpu.make_async_copy(from_s, held.at[1], sem.at[1]),
    ]
    store = [
        pltpu.make_async_copy(held.at[0], out_r, sem.at[2]),
        pltpu.make_async_copy(held.at[1], out_s, sem.at[3]),
    ]
    for one in fetch:
        one.start()
    for one, after in zip(fetch, store):
        one.wait()
        after.start()
    for one in store:
        one.wait()


def solution(mesh):
    ring, band = mesh.shape["circ"], mesh.shape["span"]

    def per_device(
        adjoint_rotor,
        adjoint_stator,
        jac_diag_rotor,
        jac_diag_stator,
        jac_off_rotor,
        jac_off_stator,
        source_rotor,
        source_stator,
        rotor_state,
        margin_block,
        face_count,
        margin_weight,
    ):
        f32, bf16 = jnp.float32, jnp.bfloat16
        shape = adjoint_rotor.shape
        piece = rotor_state.shape
        split = (2, 6, 2, 128)
        lists = jnp.transpose(margin_block, (0, 2, 1))
        out = jax.ShapeDtypeStruct(shape, f32)
        hbm = pl.BlockSpec(memory_space=pltpu.HBM)
        swept = pl.pallas_call(
            functools.partial(kernel, ring, band),
            out_shape=(out, out),
            in_specs=[hbm] * 12,
            out_specs=(hbm, hbm),
            scratch_shapes=[
                pltpu.VMEM((2,) + shape, f32),
                pltpu.VMEM((2,) + shape, f32),
                pltpu.VMEM((2,) + jac_off_rotor.shape, bf16),
                pltpu.VMEM((2,) + shape, f32),
                pltpu.VMEM(margin_weight.shape, f32),
                pltpu.SMEM(lists.shape, jnp.int32),
                pltpu.SMEM(face_count.shape, jnp.int32),
                pltpu.VMEM(piece, bf16),
                pltpu.VMEM((2, 6, 2, 8, 256), f32),
                pltpu.VMEM((2,) + shape, f32),
                pltpu.VMEM((2,) + shape, f32),
                pltpu.VMEM((STEPS, 2, 2, 6, 2, 4, 128), f32),
                pltpu.VMEM((STEPS, 2, 2, 6, 4, 256), f32),
                pltpu.VMEM((HOMES,) + piece, bf16),
                pltpu.VMEM((HOMES,) + split, f32),
                pltpu.VMEM((COARSE,) + piece, bf16),
                pltpu.VMEM((SLOTS,) + piece, bf16),
                pltpu.VMEM((SLOTS,) + split, f32),
                pltpu.VMEM(piece, bf16),
                pltpu.VMEM(piece, f32),
                pltpu.VMEM(piece, f32),
                pltpu.VMEM(piece, f32),
                pltpu.VMEM((COARSE,) + split, f32),
                pltpu.VMEM((COARSE,) + split, f32),
                pltpu.VMEM((SLOTS,) + split, f32),
                pltpu.VMEM((SLOTS,) + split, f32),
                pltpu.VMEM((2,) + split, f32),
                pltpu.VMEM((2,) + split, f32),
                pltpu.VMEM((2,) + split, f32),
                pltpu.VMEM((2,) + split[1:], f32),
                pltpu.VMEM((2, 6, 8, 128), f32),
                pltpu.VMEM((2, 6, 8, 128), f32),
                pltpu.VMEM((2, 6, 8, 128), f32),
                pltpu.VMEM((2, 2, 8, 128), f32),
                pltpu.VMEM((3,) + split, f32),
                pltpu.VMEM((2, 2) + split, f32),
                pltpu.VMEM((2, 2) + split[1:], f32),
                pltpu.SemaphoreType.DMA((12,)),
                pltpu.SemaphoreType.DMA((2,)),
                pltpu.SemaphoreType.DMA((STEPS, 2, 8)),
                pltpu.SemaphoreType.DMA((7,)),
                pltpu.SemaphoreType.DMA((7,)),
                pltpu.SemaphoreType.DMA((8,)),
                pltpu.SemaphoreType.DMA((2, 8)),
            ],
            compiler_params=pltpu.CompilerParams(
                collective_id=0, has_side_effects=True, vmem_limit_bytes=60 * 1024 * 1024
            ),
            name="sweep",
        )(
            adjoint_rotor,
            adjoint_stator,
            jac_diag_rotor,
            jac_diag_stator,
            jac_off_rotor,
            jac_off_stator,
            source_rotor,
            source_stator,
            rotor_state,
            lists,
            face_count,
            margin_weight,
        )
        return pl.pallas_call(
            deliver,
            out_shape=(out, out),
            in_specs=[hbm] * 2,
            out_specs=(hbm, hbm),
            scratch_shapes=[pltpu.VMEM((2,) + shape, f32), pltpu.SemaphoreType.DMA((4,))],
            compiler_params=pltpu.CompilerParams(vmem_limit_bytes=60 * 1024 * 1024),
            name="deliver",
        )(*swept)

    field = P(None, "span", None, "circ")
    matrix = P(None, None, "span", None, "circ")
    placed = (field,) * 4 + (matrix,) * 2 + (field,) * 2
    placed = placed + (
        P(None, "span", "circ"),
        P("span", None, None),
        P("span", None),
        P("span", None, None, None),
    )
    return jax.shard_map(
        per_device, mesh=mesh, in_specs=placed, out_specs=(field, field), check_vma=False
    )
```
